32 devices in a mesh: beam: 2 (over y), inp: 8 (over z, x), span: 2 (over core).
Axes of the slice: x: 2, y: 2, z: 4, core: 2. Of those that a mesh axis runs over, the one named last changes fastest.
Arguments:
- voltages: bfloat16 [2, 8, 1024, 16384], P(None, 'beam', 'inp', 'span'), parts along dimension 1, may hold values from -6 to 6
- gains: float32 [2, 8, 1024, 32], P(None, 'beam', 'inp'), parts along dimension 1, may hold values from -4 to 4
Outputs:
- visibilities: bfloat16 [256, 1024, 1024], P(('beam', 'inp'), 'span'), parts along dimension 0
The draws below stay inside these ranges and needn't reach their ends.
There are 2 independent parts, one for each index of `beam`. The reference program is written for one: setup_inputs(seed, part) draws one part's arguments, and reference() takes and returns one part's arrays. A program takes and returns all parts, laid end to end along the dimension named above; each array names one. Nothing has to cross between parts.
All inputs are finite; a program needn't handle non-finite values.
Results may differ from the reference program's by a relative error of at most 0.0085.
Values may be sent and summed in bfloat16 or wider, within the bound.
A program may use at most 192 MiB of HBM per device.

```python
import math
import jax
import jax.numpy as jnp
from jax import lax

NI = 1024
FINE = 32
TAPS = 4
COARSE = 4
FRAMES = 256
SAMPLES = 8192
SPANS = 2


def shard_levels(own_key, shape, split, low, high):
    def one(dim, shards_of):
        draws = jax.random.uniform(jax.random.fold_in(jax.random.fold_in(own_key, 6), dim), (shards_of,), jnp.float32, low / len(split), high / len(split))
        return jnp.repeat(jnp.exp(draws), shape[dim] // shards_of).reshape((-1,) + (1,) * (len(shape) - dim - 1))

    level = one(*split[0])
    for cut in split[1:]:
        level = level * one(*cut)
    return level


def bell_draw(own_key, extent, spread, most, pieces=(), held_as=jnp.bfloat16):
    values = spread * jax.random.normal(own_key, extent, jnp.float32)
    if pieces:
        values = values * shard_levels(own_key, extent, pieces, -0.22, 0.18)
    return jnp.clip(values, -most, most).astype(held_as)


def setup_inputs(seed: int = 0, part: int = 0) -> dict:
    key_list = jax.random.split(jax.random.key(seed), 3)
    own_keys = jax.random.split(jax.random.fold_in(key_list[2], part), 3)
    return {
        "voltages": bell_draw(own_keys[0], (2, COARSE, NI, SPANS * SAMPLES), 1.0, 6.0, ((2, 8), (3, 2))),
        "gains": bell_draw(own_keys[1], (2, COARSE, NI, FINE), 0.7, 4.0, ((2, 8),), jnp.float32),
    }


def prototype(tap_count, fine_count):
    length = tap_count * fine_count
    offsets = jnp.arange(length).astype(jnp.float32)
    shifted = (offsets - length / 2 + 0.5) / fine_count
    taper = 0.5 - 0.5 * jnp.cos(2.0 * math.pi * (offsets + 0.5) / length)
    window = jnp.sinc(shifted) * taper
    window = window / jnp.sqrt(jnp.sum(window * window))
    return window.reshape(tap_count, fine_count)

def kernels(window, fine_count):
    points = jnp.arange(fine_count)
    phase_steps = points[:, None] * points[None, :] % fine_count
    angles = 2.0 * math.pi * phase_steps.astype(jnp.float32) / fine_count
    cosine = jnp.cos(angles)
    sine_part = jnp.sin(angles)
    result = []
    for tap_index in range(window.shape[0]):
        weights = window[tap_index][:, None]
        hcos = weights * cosine
        hsin = weights * sine_part
        result.append(jnp.stack([jnp.stack([hcos, -hsin]), jnp.stack([hsin, hcos])]))
    return jnp.stack(result)

def reference(voltages, gains):
    window = prototype(TAPS, FINE)
    filters = kernels(window, FINE)
    frame_scale = 1.0 / (SPANS * FRAMES)

    def one_coarse(coarse_args):
        voltage_block, gain_block = coarse_args
        wide = voltage_block.astype(jnp.float32).reshape(2, NI, SPANS, SAMPLES)
        wide = jnp.pad(wide, ((0, 0), (0, 0), (0, 0), (0, (TAPS - 1) * FINE)))
        spectra = jnp.zeros((2, FINE, NI, SPANS, FRAMES), jnp.float32)
        for tap_index in range(TAPS):
            sample_piece = wide[..., tap_index * FINE:tap_index * FINE + SAMPLES]
            sample_piece = sample_piece.reshape(2, NI, SPANS, FRAMES, FINE)
            spectra = spectra + jnp.einsum('aismp,abpk->bkism', sample_piece, filters[tap_index], precision=lax.Precision.HIGHEST)
        gain_real = gain_block[0].T[:, :, None, None]
        gain_imag = gain_block[1].T[:, :, None, None]
        real_part = spectra[0] * gain_real - spectra[1] * gain_imag
        imag_part = spectra[0] * gain_imag + spectra[1] * gain_real
        return jnp.stack([real_part, imag_part]).astype(jnp.bfloat16).reshape(2, FINE, NI, SPANS * FRAMES)
    spectra_all = lax.map(one_coarse, (jnp.moveaxis(voltages, 1, 0), jnp.moveaxis(gains, 1, 0)))
    channel_data = jnp.moveaxis(spectra_all, 1, 2).reshape(COARSE * FINE, 2, NI, SPANS * FRAMES)
    row_index = jnp.arange(NI)
    upper = row_index[:, None] <= row_index[None, :]

    def one_channel(channel_spec):
        left_rows = jnp.concatenate([channel_spec[0], channel_spec[1]], axis=-1)
        right_rows = jnp.concatenate([channel_spec[1], -channel_spec[0]], axis=-1)
        real_sums = jnp.dot(left_rows, left_rows.T, preferred_element_type=jnp.float32)
        imag_sums = jnp.dot(right_rows, left_rows.T, preferred_element_type=jnp.float32)
        return jnp.where(upper, real_sums * frame_scale, imag_sums * frame_scale).astype(jnp.bfloat16)
    return lax.map(one_channel, channel_data)
```

```python
import functools
import math

import jax
import jax.numpy as jnp
import numpy as np
from jax import lax
from jax.experimental import pallas as pl
from jax.experimental.pallas import tpu as pltpu
from jax.sharding import PartitionSpec as P

FINE = 32
TAPS = 4
MESH = pl.DeviceIdType.MESH


def prototype(tap_count, fine_count):
    length = tap_count * fine_count
    offsets = jnp.arange(length).astype(jnp.float32)
    shifted = (offsets - length / 2 + 0.5) / fine_count
    taper = 0.5 - 0.5 * jnp.cos(2.0 * math.pi * (offsets + 0.5) / length)
    window = jnp.sinc(shifted) * taper
    window = window / jnp.sqrt(jnp.sum(window * window))
    return window.reshape(tap_count, fine_count)


def kernels(window, fine_count):
    points = jnp.arange(fine_count)
    phase_steps = points[:, None] * points[None, :] % fine_count
    angles = 2.0 * math.pi * phase_steps.astype(jnp.float32) / fine_count
    cosine = jnp.cos(angles)
    sine_part = jnp.sin(angles)
    result = []
    for tap_index in range(window.shape[0]):
        weights = window[tap_index][:, None]
        hcos = weights * cosine
        hsin = weights * sine_part
        result.append(jnp.stack([jnp.stack([hcos, -hsin]), jnp.stack([hsin, hcos])]))
    return jnp.stack(result)


def packed_rows(left_rows, right_rows, left_all, row_start):
    real_sums = jnp.einsum("cif,cjf->cij", left_rows, left_all, preferred_element_type=jnp.float32)
    imag_sums = jnp.einsum("cif,cjf->cij", right_rows, left_all, preferred_element_type=jnp.float32)
    row_index = row_start + jnp.arange(left_rows.shape[1])
    col_index = jnp.arange(left_all.shape[1])
    upper = row_index[:, None] <= col_index[None, :]
    return jnp.where(upper[None], real_sums, imag_sums)


def local(voltages, gains):
    coarse = voltages.shape[1]
    local_inputs = voltages.shape[2]
    samples = voltages.shape[3]
    frames = samples // FINE
    window = prototype(TAPS, FINE)
    filters = kernels(window, FINE)
    filter_table = jnp.transpose(filters, (1, 0, 3, 2, 4))
    filter_high = filter_table.astype(jnp.bfloat16)
    filter_low = (filter_table - filter_high.astype(jnp.float32)).astype(jnp.bfloat16)
    padded = jnp.pad(voltages, ((0, 0), (0, 0), (0, 0), (0, (TAPS - 1) * FINE)))
    stacked = jnp.stack(
        [padded[..., tap_index * FINE : tap_index * FINE + samples] for tap_index in range(TAPS)],
        axis=1,
    )
    stacked = stacked.reshape(2, TAPS, coarse, local_inputs, frames, FINE)
    spectra = jnp.einsum(
        "atcnmp,atpbk->bcknm", stacked, filter_high, preferred_element_type=jnp.float32
    )
    spectra = spectra + jnp.einsum(
        "atcnmp,atpbk->bcknm", stacked, filter_low, preferred_element_type=jnp.float32
    )
    gain_real = jnp.swapaxes(gains[0], 1, 2)[:, :, :, None]
    gain_imag = jnp.swapaxes(gains[1], 1, 2)[:, :, :, None]
    real_part = spectra[0] * gain_real - spectra[1] * gain_imag
    imag_part = spectra[0] * gain_imag + spectra[1] * gain_real
    outgoing = jnp.stack([real_part, imag_part]).astype(jnp.bfloat16)
    outgoing = outgoing.reshape(2, coarse * FINE, local_inputs, frames)
    turned = lax.all_to_all(outgoing, "inp", split_axis=1, concat_axis=2, tiled=True)
    inputs = turned.shape[2]
    span_count = lax.axis_size("span")
    row_count = inputs // span_count
    frame_scale = 1.0 / (span_count * frames)
    row_start = lax.axis_index("span") * row_count
    frame_piece = lax.all_gather(turned, "span", axis=3, tiled=True)
    left_all = jnp.concatenate([frame_piece[0], frame_piece[1]], axis=-1)
    own_rows = lax.dynamic_slice_in_dim(frame_piece, row_start, row_count, 2)
    left_rows = jnp.concatenate([own_rows[0], own_rows[1]], axis=-1)
    right_rows = jnp.concatenate([own_rows[1], -own_rows[0]], axis=-1)
    summed = packed_rows(left_rows, right_rows, left_all, row_start) * frame_scale
    return summed.astype(jnp.bfloat16)


def order_of(step, mine, coarse):
    if coarse == 4:
        high = (mine // 2 + 1 - step // 2) % 2
        low = (mine % 2 + (step + 1) // 2) % 2
        return 2 * high + low
    return (mine + step + 1) % coarse


def origin_of(step, mine, coarse):
    if coarse == 4:
        return order_of(step, mine, coarse)
    return (mine + coarse - (step + 1) % coarse) % coarse


def filter_rows(fine_count, tap_count, group):
    length = tap_count * fine_count
    offsets = np.arange(length, dtype=np.float64)
    shifted = (offsets - length / 2 + 0.5) / fine_count
    taper = 0.5 - 0.5 * np.cos(2.0 * np.pi * (offsets + 0.5) / length)
    window = np.sinc(shifted) * taper
    window = window / np.sqrt(np.sum(window * window))
    fine = np.arange(fine_count)
    angles = 2.0 * np.pi * ((offsets[None, :] * fine[:, None]) % fine_count) / fine_count
    hcos = window[None, :] * np.cos(angles)
    hsin = window[None, :] * np.sin(angles)
    span = group * fine_count + length
    rows = np.zeros((group, 2, fine_count, 2, span), np.float64)
    for frame in range(group):
        at = slice(frame * fine_count, frame * fine_count + length)
        rows[frame, 0, :, 0, at] = hcos
        rows[frame, 0, :, 1, at] = hsin
        rows[frame, 1, :, 0, at] = -hsin
        rows[frame, 1, :, 1, at] = hcos
    rows = rows.reshape(group * 2 * fine_count, 2 * span).astype(np.float32)
    high = rows.astype(jnp.bfloat16)
    low = (rows - high.astype(np.float32)).astype(jnp.bfloat16)
    return high, low


def products(dims, span, source, turned, result):
    ranks, _, _, local_inputs, frames, _, scale = dims
    rows = ranks * local_inputs // 2
    own_sources = ranks // 2
    depth = 2 * frames
    width = 2 * local_inputs

    def turn_over(part):
        @pl.loop(0, own_sources)
        def _(index):
            at = pl.ds(pl.multiple_of(index * local_inputs, local_inputs), local_inputs)
            where_real = pl.ds(pl.multiple_of(part * frames, frames), frames)
            where_imag = pl.ds(pl.multiple_of(depth + part * frames, frames), frames)
            real = source[part, span * own_sources + index, 0].T
            imag = source[part, span * own_sources + index, 1].T
            turned[0, at, where_real] = real
            turned[0, at, where_imag] = imag
            turned[1, at, where_real] = imag
            turned[1, at, where_imag] = -real

    def columns_of(pair):
        columns = []
        for side in range(2):
            other = pair * 2 + side
            columns.append(
                jnp.concatenate(
                    [source[part, other, piece] for piece in range(2) for part in range(2)], axis=0
                )
            )
        return jnp.concatenate(columns, axis=1)

    def multiply(index):
        @pl.loop(0, ranks // 4)
        def _(step):
            pair = (1 - span) * (ranks // 4) + step
            block = columns_of(pair)
            value = jnp.dot(turned[span], block, preferred_element_type=jnp.float32) * scale
            at = pl.multiple_of(pair * width, width)
            result[index, :, pl.ds(at, width)] = value.astype(jnp.bfloat16)

        @pl.loop(0, ranks // 4)
        def _(step):
            pair = span * (ranks // 4) + step
            block = columns_of(pair)
            real = jnp.dot(turned[0], block, preferred_element_type=jnp.float32)
            imag = jnp.dot(turned[1], block, preferred_element_type=jnp.float32)
            row = lax.broadcasted_iota(jnp.int32, (rows, width), 0)
            column = step * width + lax.broadcasted_iota(jnp.int32, (rows, width), 1)
            value = jnp.where(row <= column, real, imag) * scale
            at = pl.multiple_of(pair * width, width)
            result[index, :, pl.ds(at, width)] = value.astype(jnp.bfloat16)

    return turn_over, multiply


def finish_kernel(dims, done, last, vis, turned, obuf, outsem, osem):
    chunks = dims[2]
    span = lax.axis_index("span")
    turn_over, multiply = products(dims, span, last, turned, obuf)

    def give(channel):
        return pltpu.make_async_copy(done.at[channel], vis.at[channel], outsem.at[channel])

    for channel in range(chunks - 1):
        give(channel).start()
    for part in range(2):
        turn_over(part)
    multiply(0)
    result = pltpu.make_async_copy(obuf.at[0], vis.at[chunks - 1], osem)
    result.start()
    for channel in range(chunks - 1):
        give(channel).wait()
    result.wait()


def fused_kernel(
    dims, volt, gains_in, filters_in, vis, recv, last,
    send, xbuf, tbuf, filters, gains, bbuf, turned,
    xsem, fsem, gsem, ownsem, ssem, lssem, rsem, firstsem, lrsem, psend, precv, plsend, plrecv, bsem,
):
    ranks, coarse, chunks, local_inputs, frames, first, scale = dims
    halves = ranks // coarse
    samples = frames * FINE
    rest = frames - first
    many = chunks - 1
    beam = lax.axis_index("beam")
    me = lax.axis_index("inp")
    span = lax.axis_index("span")
    mine = me // halves
    my_half = me % halves
    here = (beam, me, 1 - span)

    def peer(step, turn):
        return order_of(step, mine, coarse) * halves + (my_half + turn) % halves

    def source(step, turn):
        return origin_of(step, mine, coarse) * halves + (my_half + turn) % halves

    peers = [(step, turn) for step in range(coarse) for turn in range(halves)]
    peers = [pair for pair in peers if pair != (coarse - 1, 0)]

    barrier = pltpu.get_barrier_semaphore()
    for step, turn in peers:
        pl.semaphore_signal(barrier, inc=1, device_id=(beam, peer(step, turn), span), device_id_type=MESH)
    pl.semaphore_signal(barrier, inc=1, device_id=here, device_id_type=MESH)

    early = first * FINE + TAPS * FINE

    def load(step, slot, piece=None):
        block = order_of(step, mine, coarse)
        at = pl.ds(0, samples) if piece is None else (pl.ds(0, early), pl.ds(early, samples - early))[piece]
        return pltpu.make_async_copy(
            volt.at[:, block, :, at], xbuf.at[slot, :, :, at], xsem.at[slot if piece is None else 2 * piece]
        )

    load(0, 0, 0).start()
    take_filters = pltpu.make_async_copy(filters_in, filters, fsem)
    take_gains = pltpu.make_async_copy(gains_in, gains, gsem)
    take_filters.start()
    take_gains.start()
    load(0, 0, 1).start()
    if coarse > 1:
        load(1, 1).start()

    tail = jnp.zeros((2, local_inputs, TAPS * FINE), jnp.bfloat16)
    xbuf[0, :, :, pl.ds(samples, TAPS * FINE)] = tail
    xbuf[1, :, :, pl.ds(samples, TAPS * FINE)] = tail

    def remote(step, turn, src, dst, send_sem, recv_sem):
        return pltpu.make_async_remote_copy(
            src_ref=src, dst_ref=dst, send_sem=send_sem, recv_sem=recv_sem,
            device_id=(beam, peer(step, turn), span), device_id_type=MESH,
        )

    def span_of(step):
        return pl.ds(first, rest) if step == 0 else pl.ds(0, frames)

    def outgoing(step, turn, chunk):
        other, at = peer(step, turn), span_of(step)
        return remote(
            step, turn, send.at[other, chunk, :, at], recv.at[span, chunk, me, :, at],
            ssem.at[other], rsem.at[chunk, me],
        )

    def outgoing_last(step, turn, at=None):
        other, at = peer(step, turn), span_of(step) if at is None else at
        return remote(
            step, turn, send.at[other, many, :, at], last.at[span, me, :, at], lssem.at[other], lrsem.at[me]
        )

    def outgoing_first(turn):
        other, at = peer(0, turn), pl.ds(0, first)
        return remote(
            0, turn, send.at[other, pl.ds(0, many), :, at], recv.at[span, :, me, :, at],
            ssem.at[other], firstsem.at[me],
        )

    def sent(step, turn):
        other = peer(step, turn)
        return remote(
            step, turn, send.at[other, pl.ds(0, many)], recv.at[span, :, me], ssem.at[other], firstsem.at[me]
        )

    def incoming(step, turn, chunk):
        other, at = source(step, turn), span_of(step)
        return remote(
            step, turn, recv.at[span, chunk, other, :, at], recv.at[span, chunk, other, :, at],
            ssem.at[other], rsem.at[chunk, other],
        )

    def incoming_first(turn):
        other, at = source(0, turn), pl.ds(0, first)
        return remote(
            0, turn, recv.at[span, :, other, :, at], recv.at[span, :, other, :, at],
            ssem.at[other], firstsem.at[other],
        )

    def incoming_last(other):
        return remote(0, 0, last.at[span, other], last.at[span, other], lssem.at[other], lrsem.at[other])

    def across(ref, send_sem, recv_sem):
        return pltpu.make_async_remote_copy(
            src_ref=ref, dst_ref=ref, send_sem=send_sem, recv_sem=recv_sem,
            device_id=here, device_id_type=MESH,
        )

    def channelize(slot, start, count):
        @pl.loop(0, count // 8, unroll=2)
        def _(pair):
            base = pl.multiple_of(start * FINE + pair * (8 * FINE), 4 * FINE)
            pieces = []
            for part in range(2):
                at = base + part * 4 * FINE
                at = pl.multiple_of(at, 4 * FINE)
                pieces.append(
                    jnp.concatenate(
                        [xbuf[slot, 0, :, pl.ds(at, 8 * FINE)], xbuf[slot, 1, :, pl.ds(at, 8 * FINE)]],
                        axis=1,
                    )
                )
            both = jnp.concatenate(pieces, axis=0)
            contract = (((1,), (1,)), ((), ()))
            got = lax.dot_general(filters[0], both, contract, preferred_element_type=jnp.float32)
            got = got + lax.dot_general(filters[1], both, contract, preferred_element_type=jnp.float32)
            at = pl.multiple_of(pair * (16 * FINE), 16 * FINE)
            tbuf[pl.ds(at, 8 * FINE), :] = got[:, :local_inputs]
            tbuf[pl.ds(at + 8 * FINE, 8 * FINE), :] = got[:, local_inputs:]

    def weigh(step, turn, start, count):
        block = order_of(step, mine, coarse)
        half = (my_half + turn) % halves
        other = peer(step, turn)

        @pl.loop(0, chunks, unroll=2)
        def _(chunk):
            fine = half * chunks + chunk
            real = tbuf[pl.ds(fine, count, stride=2 * FINE), :]
            imag = tbuf[pl.ds(FINE + fine, count, stride=2 * FINE), :]
            gain_real = gains[0, block, pl.ds(fine, 1), :]
            gain_imag = gains[1, block, pl.ds(fine, 1), :]
            at = pl.ds(start, count)
            send[other, chunk, 0, at] = (real * gain_real - imag * gain_imag).astype(jnp.bfloat16)
            send[other, chunk, 1, at] = (real * gain_imag + imag * gain_real).astype(jnp.bfloat16)

    load(0, 0, 0).wait()
    take_filters.wait()
    channelize(0, 0, first)
    take_gains.wait()
    for turn in range(halves):
        weigh(0, turn, 0, first)
        if turn == 0:
            pl.semaphore_wait(barrier, len(peers) + 1)
        if (0, turn) in peers:
            outgoing_first(turn).start()
            outgoing_last(0, turn, pl.ds(0, first)).start()
    for step in range(coarse):
        slot = step % 2
        start = first if step == 0 else 0
        if step == 0:
            load(0, 0, 1).wait()
        else:
            load(step, slot).wait()
        channelize(slot, start, frames - start)
        if step + 2 < coarse:
            load(step + 2, slot).start()
        for turn in range(halves):
            weigh(step, turn, start, frames - start)
            if (step, turn) in peers:

                @pl.loop(0, many)
                def _(chunk):
                    outgoing(step, turn, chunk).start()

                outgoing_last(step, turn).start()
            else:
                own = pltpu.make_async_copy(send.at[me, pl.ds(0, many)], recv.at[span, :, me], ownsem.at[0])
                own_last = pltpu.make_async_copy(send.at[me, many], last.at[span, me], ownsem.at[1])
                own.start()
                own_last.start()
    own.wait()
    own_last.wait()

    for turn in range(halves):
        if (0, turn) in peers:
            incoming_first(turn).wait_recv()

    def forward(chunk):
        return across(recv.at[span, chunk], psend.at[0], precv.at[chunk])

    def backward(chunk):
        return across(recv.at[1 - span, chunk], psend.at[0], precv.at[chunk])

    def fetch(chunk, part):
        return pltpu.make_async_copy(recv.at[part, chunk], bbuf.at[part], bsem.at[part])

    turn_over, multiply = products(dims, span, bbuf, turned, vis)

    @pl.loop(0, many)
    def _(chunk):
        for step, turn in peers:
            incoming(step, turn, chunk).wait_recv()
        forward(chunk).start()
        fetch(chunk, span).start()
        fetch(chunk, span).wait()
        turn_over(span)
        backward(chunk).wait_recv()
        fetch(chunk, 1 - span).start()
        fetch(chunk, 1 - span).wait()
        turn_over(1 - span)
        multiply(chunk)

    def forward_last(other):
        return across(last.at[span, other], plsend.at[other], plrecv.at[other])

    def backward_last(other):
        return across(last.at[1 - span, other], plsend.at[other], plrecv.at[other])

    inner = (mine // 2 + mine % 2) % 2
    pairs = [(source(0, turn), source(1, turn)) for turn in range(halves)]
    final = [source(step, turn) for step, turn in peers if step > 1]
    final += [inner * one + (1 - inner) * other for one, other in pairs]
    final += [(1 - inner) * one + inner * other for one, other in pairs]
    forward_last(me).start()
    for other in final:
        incoming_last(other).wait_recv()
        forward_last(other).start()
    for step, turn in peers:
        sent(step, turn).wait_send()
        outgoing_last(step, turn, pl.ds(0, frames)).wait_send()
    across(recv.at[span], psend.at[0], precv.at[0]).wait_send()
    for other in [me] + final:
        forward_last(other).wait_send()
        backward_last(other).wait_recv()


def fused(voltages, gains):
    coarse, local_inputs, samples = voltages.shape[1:]
    ranks = lax.axis_size("inp")
    frames = samples // FINE
    halves = ranks // coarse
    chunks = FINE // halves
    rows = ranks * local_inputs // 2
    columns = ranks * local_inputs
    first = 32
    filters = jnp.asarray(np.stack(filter_rows(FINE, TAPS, 4)))
    gain_rows = jnp.swapaxes(gains, 2, 3)
    scale = 1.0 / (2 * frames)
    dims = (ranks, coarse, chunks, local_inputs, frames, first, scale)
    bf16 = jnp.bfloat16
    anywhere = pl.BlockSpec(memory_space=pl.ANY)
    inside = pl.BlockSpec(memory_space=pltpu.VMEM)
    flops = 4 * chunks * rows * columns * 4 * frames
    done, _, last = pl.pallas_call(
        functools.partial(fused_kernel, dims),
        out_shape=(
            pltpu.VMEM((chunks - 1, rows, columns), bf16),
            jax.ShapeDtypeStruct((2, chunks - 1, ranks, 2, frames, local_inputs), bf16),
            pltpu.VMEM((2, ranks, 2, frames, local_inputs), bf16),
        ),
        in_specs=[anywhere, anywhere, anywhere],
        out_specs=(inside, anywhere, inside),
        scratch_shapes=[
            pltpu.VMEM((ranks, chunks, 2, frames, local_inputs), bf16),
            pltpu.VMEM((2, 2, local_inputs, samples + TAPS * FINE), bf16),
            pltpu.VMEM((frames * 2 * FINE, local_inputs), jnp.float32),
            pltpu.VMEM(filters.shape, bf16),
            pltpu.VMEM(gain_rows.shape, jnp.float32),
            pltpu.VMEM((2, ranks, 2, frames, local_inputs), bf16),
            pltpu.VMEM((2, rows, 4 * frames), bf16),
            pltpu.SemaphoreType.DMA((3,)),
            pltpu.SemaphoreType.DMA,
            pltpu.SemaphoreType.DMA,
            pltpu.SemaphoreType.DMA((2,)),
            pltpu.SemaphoreType.DMA((ranks,)),
            pltpu.SemaphoreType.DMA((ranks,)),
            pltpu.SemaphoreType.DMA((chunks - 1, ranks)),
            pltpu.SemaphoreType.DMA((ranks,)),
            pltpu.SemaphoreType.DMA((ranks,)),
            pltpu.SemaphoreType.DMA((1,)),
            pltpu.SemaphoreType.DMA((chunks - 1,)),
            pltpu.SemaphoreType.DMA((ranks,)),
            pltpu.SemaphoreType.DMA((ranks,)),
            pltpu.SemaphoreType.DMA((2,)),
        ],
        compiler_params=pltpu.CompilerParams(
            collective_id=0, has_side_effects=True, vmem_limit_bytes=44 * 1024 * 1024
        ),
        cost_estimate=pl.CostEstimate(flops=flops, bytes_accessed=2 * voltages.size * 8, transcendentals=0),
    )(voltages, gain_rows, filters)
    done = pltpu.with_memory_space_constraint(done, pltpu.VMEM)
    last = pltpu.with_memory_space_constraint(last, pltpu.VMEM)
    return pl.pallas_call(
        functools.partial(finish_kernel, dims),
        out_shape=jax.ShapeDtypeStruct((chunks, rows, columns), bf16),
        in_specs=[inside, inside],
        out_specs=anywhere,
        scratch_shapes=[
            pltpu.VMEM((2, rows, 4 * frames), bf16),
            pltpu.VMEM((1, rows, columns), bf16),
            pltpu.SemaphoreType.DMA((chunks - 1,)),
            pltpu.SemaphoreType.DMA,
        ],
        compiler_params=pltpu.CompilerParams(vmem_limit_bytes=24 * 1024 * 1024),
    )(done, last)


def vmem_needed(coarse, local_inputs, samples, ranks):
    frames = samples // FINE
    chunks = FINE * coarse // ranks
    spectra = 4 * frames * local_inputs
    columns = ranks * local_inputs
    kept = chunks * columns * columns + 2 * ranks * spectra
    sending = ranks * chunks * spectra
    sampled = 8 * local_inputs * (samples + TAPS * FINE)
    channelized = frames * 2 * FINE * local_inputs * 4
    correlated = 2 * ranks * spectra + columns * 4 * frames * 2
    return kept, sending + sampled + channelized + correlated


def chosen(voltages, gains):
    coarse, local_inputs, samples = voltages.shape[1:]
    ranks, spans = lax.axis_size("inp"), lax.axis_size("span")
    fits = (
        spans == 2
        and local_inputs % 128 == 0
        and coarse > 2
        and ranks % coarse == 0
        and ranks % 4 == 0
        and FINE % (ranks // coarse) == 0
        and samples % (16 * FINE) == 0
        and samples >= 64 * FINE
    )
    if fits:
        kept, working = vmem_needed(coarse, local_inputs, samples, ranks)
        fits = kept <= 18 * 1024 * 1024 and working <= 42 * 1024 * 1024
    return fused(voltages, gains) if fits else local(voltages, gains)


def solution(mesh):
    placed = (P(None, "beam", "inp", "span"), P(None, "beam", "inp", None))
    return jax.shard_map(
        chosen,
        mesh=mesh,
        in_specs=placed,
        out_specs=P(("beam", "inp"), "span", None),
        check_vma=False,
    )
```

```python
import functools
import math

import jax
import jax.numpy as jnp
import numpy as np
from jax import lax
from jax.experimental import pallas as pl
from jax.experimental.pallas import tpu as pltpu
from jax.sharding import PartitionSpec as P

FINE = 32
TAPS = 4
MESH = pl.DeviceIdType.MESH


def prototype(tap_count, fine_count):
    length = tap_count * fine_count
    offsets = jnp.arange(length).astype(jnp.float32)
    shifted = (offsets - length / 2 + 0.5) / fine_count
    taper = 0.5 - 0.5 * jnp.cos(2.0 * math.pi * (offsets + 0.5) / length)
    window = jnp.sinc(shifted) * taper
    window = window / jnp.sqrt(jnp.sum(window * window))
    return window.reshape(tap_count, fine_count)


def kernels(window, fine_count):
    points = jnp.arange(fine_count)
    phase_steps = points[:, None] * points[None, :] % fine_count
    angles = 2.0 * math.pi * phase_steps.astype(jnp.float32) / fine_count
    cosine = jnp.cos(angles)
    sine_part = jnp.sin(angles)
    result = []
    for tap_index in range(window.shape[0]):
        weights = window[tap_index][:, None]
        hcos = weights * cosine
        hsin = weights * sine_part
        result.append(jnp.stack([jnp.stack([hcos, -hsin]), jnp.stack([hsin, hcos])]))
    return jnp.stack(result)


def packed_rows(left_rows, right_rows, left_all, row_start):
    real_sums = jnp.einsum("cif,cjf->cij", left_rows, left_all, preferred_element_type=jnp.float32)
    imag_sums = jnp.einsum("cif,cjf->cij", right_rows, left_all, preferred_element_type=jnp.float32)
    row_index = row_start + jnp.arange(left_rows.shape[1])
    col_index = jnp.arange(left_all.shape[1])
    upper = row_index[:, None] <= col_index[None, :]
    return jnp.where(upper[None], real_sums, imag_sums)


def local(voltages, gains):
    coarse = voltages.shape[1]
    local_inputs = voltages.shape[2]
    samples = voltages.shape[3]
    frames = samples // FINE
    window = prototype(TAPS, FINE)
    filters = kernels(window, FINE)
    filter_table = jnp.transpose(filters, (1, 0, 3, 2, 4))
    filter_high = filter_table.astype(jnp.bfloat16)
    filter_low = (filter_table - filter_high.astype(jnp.float32)).astype(jnp.bfloat16)
    padded = jnp.pad(voltages, ((0, 0), (0, 0), (0, 0), (0, (TAPS - 1) * FINE)))
    stacked = jnp.stack(
        [padded[..., tap_index * FINE : tap_index * FINE + samples] for tap_index in range(TAPS)],
        axis=1,
    )
    stacked = stacked.reshape(2, TAPS, coarse, local_inputs, frames, FINE)
    spectra = jnp.einsum(
        "atcnmp,atpbk->bcknm", stacked, filter_high, preferred_element_type=jnp.float32
    )
    spectra = spectra + jnp.einsum(
        "atcnmp,atpbk->bcknm", stacked, filter_low, preferred_element_type=jnp.float32
    )
    gain_real = jnp.swapaxes(gains[0], 1, 2)[:, :, :, None]
    gain_imag = jnp.swapaxes(gains[1], 1, 2)[:, :, :, None]
    real_part = spectra[0] * gain_real - spectra[1] * gain_imag
    imag_part = spectra[0] * gain_imag + spectra[1] * gain_real
    outgoing = jnp.stack([real_part, imag_part]).astype(jnp.bfloat16)
    outgoing = outgoing.reshape(2, coarse * FINE, local_inputs, frames)
    turned = lax.all_to_all(outgoing, "inp", split_axis=1, concat_axis=2, tiled=True)
    inputs = turned.shape[2]
    span_count = lax.axis_size("span")
    row_count = inputs // span_count
    frame_scale = 1.0 / (span_count * frames)
    row_start = lax.axis_index("span") * row_count
    frame_piece = lax.all_gather(turned, "span", axis=3, tiled=True)
    left_all = jnp.concatenate([frame_piece[0], frame_piece[1]], axis=-1)
    own_rows = lax.dynamic_slice_in_dim(frame_piece, row_start, row_count, 2)
    left_rows = jnp.concatenate([own_rows[0], own_rows[1]], axis=-1)
    right_rows = jnp.concatenate([own_rows[1], -own_rows[0]], axis=-1)
    summed = packed_rows(left_rows, right_rows, left_all, row_start) * frame_scale
    return summed.astype(jnp.bfloat16)


def order_of(step, mine, coarse):
    if coarse == 4:
        high = (mine // 2 + 1 - step // 2) % 2
        low = (mine % 2 + (step + 1) // 2) % 2
        return 2 * high + low
    return (mine + step + 1) % coarse


def origin_of(step, mine, coarse):
    if coarse == 4:
        return order_of(step, mine, coarse)
    return (mine + coarse - (step + 1) % coarse) % coarse


def filter_rows(fine_count, tap_count, group):
    length = tap_count * fine_count
    offsets = np.arange(length, dtype=np.float64)
    shifted = (offsets - length / 2 + 0.5) / fine_count
    taper = 0.5 - 0.5 * np.cos(2.0 * np.pi * (offsets + 0.5) / length)
    window = np.sinc(shifted) * taper
    window = window / np.sqrt(np.sum(window * window))
    fine = np.arange(fine_count)
    angles = 2.0 * np.pi * ((offsets[None, :] * fine[:, None]) % fine_count) / fine_count
    hcos = window[None, :] * np.cos(angles)
    hsin = window[None, :] * np.sin(angles)
    span = group * fine_count + length
    rows = np.zeros((group, 2, fine_count, 2, span), np.float64)
    for frame in range(group):
        at = slice(frame * fine_count, frame * fine_count + length)
        rows[frame, 0, :, 0, at] = hcos
        rows[frame, 0, :, 1, at] = hsin
        rows[frame, 1, :, 0, at] = -hsin
        rows[frame, 1, :, 1, at] = hcos
    rows = rows.reshape(group * 2 * fine_count, 2 * span).astype(np.float32)
    high = rows.astype(jnp.bfloat16)
    low = (rows - high.astype(np.float32)).astype(jnp.bfloat16)
    return high, low


def products(dims, span, source, turned, result):
    ranks, _, _, local_inputs, frames, _, scale = dims
    rows = ranks * local_inputs // 2
    own_sources = ranks // 2
    depth = 2 * frames
    width = 2 * local_inputs

    def turn_over(part):
        @pl.loop(0, own_sources)
        def _(index):
            at = pl.ds(pl.multiple_of(index * local_inputs, local_inputs), local_inputs)
            where_real = pl.ds(pl.multiple_of(part * frames, frames), frames)
            where_imag = pl.ds(pl.multiple_of(depth + part * frames, frames), frames)
            real = source[part, span * own_sources + index, 0].T
            imag = source[part, span * own_sources + index, 1].T
            turned[0, at, where_real] = real
            turned[0, at, where_imag] = imag
            turned[1, at, where_real] = imag
            turned[1, at, where_imag] = -real

    def columns_of(pair):
        columns = []
        for side in range(2):
            other = pair * 2 + side
            columns.append(
                jnp.concatenate(
                    [source[part, other, piece] for piece in range(2) for part in range(2)], axis=0
                )
            )
        return jnp.concatenate(columns, axis=1)

    def multiply(index):
        @pl.loop(0, ranks // 4)
        def _(step):
            pair = (1 - span) * (ranks // 4) + step
            block = columns_of(pair)
            value = jnp.dot(turned[span], block, preferred_element_type=jnp.float32) * scale
            at = pl.multiple_of(pair * width, width)
            result[index, :, pl.ds(at, width)] = value.astype(jnp.bfloat16)

        @pl.loop(0, ranks // 4)
        def _(step):
            pair = span * (ranks // 4) + step
            block = columns_of(pair)
            real = jnp.dot(turned[0], block, preferred_element_type=jnp.float32)
            imag = jnp.dot(turned[1], block, preferred_element_type=jnp.float32)
            row = lax.broadcasted_iota(jnp.int32, (rows, width), 0)
            column = step * width + lax.broadcasted_iota(jnp.int32, (rows, width), 1)
            value = jnp.where(row <= column, real, imag) * scale
            at = pl.multiple_of(pair * width, width)
            result[index, :, pl.ds(at, width)] = value.astype(jnp.bfloat16)

    return turn_over, multiply


def finish_kernel(dims, done, last, vis, turned, obuf, outsem, osem):
    chunks = dims[2]
    span = lax.axis_index("span")
    turn_over, multiply = products(dims, span, last, turned, obuf)

    def give(channel):
        return pltpu.make_async_copy(done.at[channel], vis.at[channel], outsem.at[channel])

    for channel in range(chunks - 1):
        give(channel).start()
    for part in range(2):
        turn_over(part)
    multiply(0)
    result = pltpu.make_async_copy(obuf.at[0], vis.at[chunks - 1], osem)
    result.start()
    for channel in range(chunks - 1):
        give(channel).wait()
    result.wait()


def fused_kernel(
    dims, volt, gains_in, filters_in, vis, recv, last,
    send, xbuf, tbuf, filters, gains, bbuf, turned,
    xsem, fsem, gsem, ownsem, ssem, lssem, rsem, firstsem, lrsem, psend, precv, plsend, plrecv, bsem,
):
    ranks, coarse, chunks, local_inputs, frames, first, scale = dims
    halves = ranks // coarse
    samples = frames * FINE
    rest = frames - first
    many = chunks - 1
    ahead = min(8, many)
    early_chunks = min(4, ahead)
    beam = lax.axis_index("beam")
    me = lax.axis_index("inp")
    span = lax.axis_index("span")
    mine = me // halves
    my_half = me % halves
    here = (beam, me, 1 - span)

    def peer(step, turn):
        return order_of(step, mine, coarse) * halves + (my_half + turn) % halves

    def source(step, turn):
        return origin_of(step, mine, coarse) * halves + (my_half + turn) % halves

    peers = [(step, turn) for step in range(coarse) for turn in range(halves)]
    peers = [pair for pair in peers if pair != (coarse - 1, 0)]

    barrier = pltpu.get_barrier_semaphore()
    for step, turn in peers:
        pl.semaphore_signal(barrier, inc=1, device_id=(beam, peer(step, turn), span), device_id_type=MESH)
    pl.semaphore_signal(barrier, inc=1, device_id=here, device_id_type=MESH)

    early = first * FINE + TAPS * FINE

    def load(step, slot, piece=None):
        block = order_of(step, mine, coarse)
        at = pl.ds(0, samples) if piece is None else (pl.ds(0, early), pl.ds(early, samples - early))[piece]
        return pltpu.make_async_copy(
            volt.at[:, block, :, at], xbuf.at[slot, :, :, at], xsem.at[slot if piece is None else 2 * piece]
        )

    load(0, 0, 0).start()
    take_filters = pltpu.make_async_copy(filters_in, filters, fsem)
    take_gains = pltpu.make_async_copy(gains_in, gains, gsem)
    take_filters.start()
    take_gains.start()
    load(0, 0, 1).start()
    if coarse > 1:
        load(1, 1).start()

    tail = jnp.zeros((2, local_inputs, TAPS * FINE), jnp.bfloat16)
    xbuf[0, :, :, pl.ds(samples, TAPS * FINE)] = tail
    xbuf[1, :, :, pl.ds(samples, TAPS * FINE)] = tail

    def remote(step, turn, src, dst, send_sem, recv_sem):
        return pltpu.make_async_remote_copy(
            src_ref=src, dst_ref=dst, send_sem=send_sem, recv_sem=recv_sem,
            device_id=(beam, peer(step, turn), span), device_id_type=MESH,
        )

    def span_of(step):
        return pl.ds(first, rest) if step == 0 else pl.ds(0, frames)

    def outgoing(step, turn, chunk):
        other, at = peer(step, turn), span_of(step)
        return remote(
            step, turn, send.at[other, chunk, :, at], recv.at[span, chunk, me, :, at],
            ssem.at[other], rsem.at[chunk, me],
        )

    def outgoing_last(step, turn, at=None):
        other, at = peer(step, turn), span_of(step) if at is None else at
        return remote(
            step, turn, send.at[other, many, :, at], last.at[span, me, :, at], lssem.at[other], lrsem.at[me]
        )

    def outgoing_first(turn):
        other, at = peer(0, turn), pl.ds(0, first)
        return remote(
            0, turn, send.at[other, pl.ds(0, many), :, at], recv.at[span, :, me, :, at],
            ssem.at[other], firstsem.at[me],
        )

    def sent(step, turn):
        other = peer(step, turn)
        return remote(
            step, turn, send.at[other, pl.ds(0, many)], recv.at[span, :, me], ssem.at[other], firstsem.at[me]
        )

    def incoming(step, turn, chunk):
        other, at = source(step, turn), span_of(step)
        return remote(
            step, turn, recv.at[span, chunk, other, :, at], recv.at[span, chunk, other, :, at],
            ssem.at[other], rsem.at[chunk, other],
        )

    def incoming_first(turn):
        other, at = source(0, turn), pl.ds(0, first)
        return remote(
            0, turn, recv.at[span, :, other, :, at], recv.at[span, :, other, :, at],
            ssem.at[other], firstsem.at[other],
        )

    def incoming_last(other):
        return remote(0, 0, last.at[span, other], last.at[span, other], lssem.at[other], lrsem.at[other])

    def across(ref, send_sem, recv_sem):
        return pltpu.make_async_remote_copy(
            src_ref=ref, dst_ref=ref, send_sem=send_sem, recv_sem=recv_sem,
            device_id=here, device_id_type=MESH,
        )

    def channelize(slot, start, count):
        @pl.loop(0, count // 8, unroll=2)
        def _(pair):
            base = pl.multiple_of(start * FINE + pair * (8 * FINE), 4 * FINE)
            pieces = []
            for part in range(2):
                at = base + part * 4 * FINE
                at = pl.multiple_of(at, 4 * FINE)
                pieces.append(
                    jnp.concatenate(
                        [xbuf[slot, 0, :, pl.ds(at, 8 * FINE)], xbuf[slot, 1, :, pl.ds(at, 8 * FINE)]],
                        axis=1,
                    )
                )
            both = jnp.concatenate(pieces, axis=0)
            contract = (((1,), (1,)), ((), ()))
            got = lax.dot_general(filters[0], both, contract, preferred_element_type=jnp.float32)
            got = got + lax.dot_general(filters[1], both, contract, preferred_element_type=jnp.float32)
            at = pl.multiple_of(pair * (16 * FINE), 16 * FINE)
            tbuf[pl.ds(at, 8 * FINE), :] = got[:, :local_inputs]
            tbuf[pl.ds(at + 8 * FINE, 8 * FINE), :] = got[:, local_inputs:]

    def weigh(step, turn, start, count):
        block = order_of(step, mine, coarse)
        half = (my_half + turn) % halves
        other = peer(step, turn)

        @pl.loop(0, chunks, unroll=2)
        def _(chunk):
            fine = half * chunks + chunk
            real = tbuf[pl.ds(fine, count, stride=2 * FINE), :]
            imag = tbuf[pl.ds(FINE + fine, count, stride=2 * FINE), :]
            gain_real = gains[0, block, pl.ds(fine, 1), :]
            gain_imag = gains[1, block, pl.ds(fine, 1), :]
            at = pl.ds(start, count)
            send[other, chunk, 0, at] = (real * gain_real - imag * gain_imag).astype(jnp.bfloat16)
            send[other, chunk, 1, at] = (real * gain_imag + imag * gain_real).astype(jnp.bfloat16)

    load(0, 0, 0).wait()
    take_filters.wait()
    channelize(0, 0, first)
    take_gains.wait()
    for turn in range(halves):
        weigh(0, turn, 0, first)
        if turn == 0:
            pl.semaphore_wait(barrier, len(peers) + 1)
        if (0, turn) in peers:
            outgoing_first(turn).start()
            outgoing_last(0, turn, pl.ds(0, first)).start()
    for step in range(coarse):
        slot = step % 2
        start = first if step == 0 else 0
        if step == 0:
            load(0, 0, 1).wait()
        else:
            load(step, slot).wait()
        channelize(slot, start, frames - start)
        if step + 2 < coarse:
            load(step + 2, slot).start()
        for turn in range(halves):
            weigh(step, turn, start, frames - start)
            if (step, turn) in peers:

                for chunk in range(early_chunks):
                    outgoing(step, turn, chunk).start()
            else:
                own = pltpu.make_async_copy(send.at[me, pl.ds(0, many)], recv.at[span, :, me], ownsem.at[0])
                own_last = pltpu.make_async_copy(send.at[me, many], last.at[span, me], ownsem.at[1])
                own.start()
                own_last.start()
    for chunk in range(early_chunks, ahead):
        for step, turn in peers:
            outgoing(step, turn, chunk).start()
    own.wait()
    own_last.wait()

    for turn in range(halves):
        if (0, turn) in peers:
            incoming_first(turn).wait_recv()

    def forward(chunk):
        return across(recv.at[span, chunk], psend.at[0], precv.at[chunk])

    def backward(chunk):
        return across(recv.at[1 - span, chunk], psend.at[0], precv.at[chunk])

    def fetch(chunk, part):
        return pltpu.make_async_copy(recv.at[part, chunk], bbuf.at[part], bsem.at[part])

    turn_over, multiply = products(dims, span, bbuf, turned, vis)

    @pl.loop(0, many)
    def _(chunk):
        for step, turn in peers:
            incoming(step, turn, chunk).wait_recv()
        forward(chunk).start()

        @pl.when(chunk + ahead < many)
        def _():
            for step, turn in peers:
                outgoing(step, turn, chunk + ahead).start()

        @pl.when(chunk + ahead == many)
        def _():
            for step, turn in peers:
                outgoing_last(step, turn).start()

        fetch(chunk, span).start()
        fetch(chunk, span).wait()
        turn_over(span)
        backward(chunk).wait_recv()
        fetch(chunk, 1 - span).start()
        fetch(chunk, 1 - span).wait()
        turn_over(1 - span)
        multiply(chunk)

    def forward_last(other):
        return across(last.at[span, other], plsend.at[other], plrecv.at[other])

    def backward_last(other):
        return across(last.at[1 - span, other], plsend.at[other], plrecv.at[other])

    inner = (mine // 2 + mine % 2) % 2
    pairs = [(source(0, turn), source(1, turn)) for turn in range(halves)]
    final = [source(step, turn) for step, turn in peers if step > 1]
    final += [inner * one + (1 - inner) * other for one, other in pairs]
    final += [(1 - inner) * one + inner * other for one, other in pairs]
    forward_last(me).start()
    for other in final:
        incoming_last(other).wait_recv()
        forward_last(other).start()
    for step, turn in peers:
        sent(step, turn).wait_send()
        outgoing_last(step, turn, pl.ds(0, frames)).wait_send()
    across(recv.at[span], psend.at[0], precv.at[0]).wait_send()
    for other in [me] + final:
        forward_last(other).wait_send()
        backward_last(other).wait_recv()


def fused(voltages, gains):
    coarse, local_inputs, samples = voltages.shape[1:]
    ranks = lax.axis_size("inp")
    frames = samples // FINE
    halves = ranks // coarse
    chunks = FINE // halves
    rows = ranks * local_inputs // 2
    columns = ranks * local_inputs
    first = 32
    filters = jnp.asarray(np.stack(filter_rows(FINE, TAPS, 4)))
    gain_rows = jnp.swapaxes(gains, 2, 3)
    scale = 1.0 / (2 * frames)
    dims = (ranks, coarse, chunks, local_inputs, frames, first, scale)
    bf16 = jnp.bfloat16
    anywhere = pl.BlockSpec(memory_space=pl.ANY)
    inside = pl.BlockSpec(memory_space=pltpu.VMEM)
    flops = 4 * chunks * rows * columns * 4 * frames
    done, _, last = pl.pallas_call(
        functools.partial(fused_kernel, dims),
        out_shape=(
            pltpu.VMEM((chunks - 1, rows, columns), bf16),
            jax.ShapeDtypeStruct((2, chunks - 1, ranks, 2, frames, local_inputs), bf16),
            pltpu.VMEM((2, ranks, 2, frames, local_inputs), bf16),
        ),
        in_specs=[anywhere, anywhere, anywhere],
        out_specs=(inside, anywhere, inside),
        scratch_shapes=[
            pltpu.VMEM((ranks, chunks, 2, frames, local_inputs), bf16),
            pltpu.VMEM((2, 2, local_inputs, samples + TAPS * FINE), bf16),
            pltpu.VMEM((frames * 2 * FINE, local_inputs), jnp.float32),
            pltpu.VMEM(filters.shape, bf16),
            pltpu.VMEM(gain_rows.shape, jnp.float32),
            pltpu.VMEM((2, ranks, 2, frames, local_inputs), bf16),
            pltpu.VMEM((2, rows, 4 * frames), bf16),
            pltpu.SemaphoreType.DMA((3,)),
            pltpu.SemaphoreType.DMA,
            pltpu.SemaphoreType.DMA,
            pltpu.SemaphoreType.DMA((2,)),
            pltpu.SemaphoreType.DMA((ranks,)),
            pltpu.SemaphoreType.DMA((ranks,)),
            pltpu.SemaphoreType.DMA((chunks - 1, ranks)),
            pltpu.SemaphoreType.DMA((ranks,)),
            pltpu.SemaphoreType.DMA((ranks,)),
            pltpu.SemaphoreType.DMA((1,)),
            pltpu.SemaphoreType.DMA((chunks - 1,)),
            pltpu.SemaphoreType.DMA((ranks,)),
            pltpu.SemaphoreType.DMA((ranks,)),
            pltpu.SemaphoreType.DMA((2,)),
        ],
        compiler_params=pltpu.CompilerParams(
            collective_id=0, has_side_effects=True, vmem_limit_bytes=44 * 1024 * 1024
        ),
        cost_estimate=pl.CostEstimate(flops=flops, bytes_accessed=2 * voltages.size * 8, transcendentals=0),
    )(voltages, gain_rows, filters)
    done = pltpu.with_memory_space_constraint(done, pltpu.VMEM)
    last = pltpu.with_memory_space_constraint(last, pltpu.VMEM)
    return pl.pallas_call(
        functools.partial(finish_kernel, dims),
        out_shape=jax.ShapeDtypeStruct((chunks, rows, columns), bf16),
        in_specs=[inside, inside],
        out_specs=anywhere,
        scratch_shapes=[
            pltpu.VMEM((2, rows, 4 * frames), bf16),
            pltpu.VMEM((1, rows, columns), bf16),
            pltpu.SemaphoreType.DMA((chunks - 1,)),
            pltpu.SemaphoreType.DMA,
        ],
        compiler_params=pltpu.CompilerParams(vmem_limit_bytes=24 * 1024 * 1024),
    )(done, last)


def vmem_needed(coarse, local_inputs, samples, ranks):
    frames = samples // FINE
    chunks = FINE * coarse // ranks
    spectra = 4 * frames * local_inputs
    columns = ranks * local_inputs
    kept = chunks * columns * columns + 2 * ranks * spectra
    sending = ranks * chunks * spectra
    sampled = 8 * local_inputs * (samples + TAPS * FINE)
    channelized = frames * 2 * FINE * local_inputs * 4
    correlated = 2 * ranks * spectra + columns * 4 * frames * 2
    return kept, sending + sampled + channelized + correlated


def chosen(voltages, gains):
    coarse, local_inputs, samples = voltages.shape[1:]
    ranks, spans = lax.axis_size("inp"), lax.axis_size("span")
    fits = (
        spans == 2
        and local_inputs % 128 == 0
        and coarse > 2
        and ranks % coarse == 0
        and ranks % 4 == 0
        and FINE % (ranks // coarse) == 0
        and samples % (16 * FINE) == 0
        and samples >= 64 * FINE
    )
    if fits:
        kept, working = vmem_needed(coarse, local_inputs, samples, ranks)
        fits = kept <= 18 * 1024 * 1024 and working <= 42 * 1024 * 1024
    return fused(voltages, gains) if fits else local(voltages, gains)


def solution(mesh):
    placed = (P(None, "beam", "inp", "span"), P(None, "beam", "inp", None))
    return jax.shard_map(
        chosen,
        mesh=mesh,
        in_specs=placed,
        out_specs=P(("beam", "inp"), "span", None),
        check_vma=False,
    )
```

```python
import functools
import math

import jax
import jax.numpy as jnp
import numpy as np
from jax import lax
from jax.experimental import pallas as pl
from jax.experimental.pallas import tpu as pltpu
from jax.sharding import PartitionSpec as P

FINE = 32
TAPS = 4
MESH = pl.DeviceIdType.MESH


def prototype(tap_count, fine_count):
    length = tap_count * fine_count
    offsets = jnp.arange(length).astype(jnp.float32)
    shifted = (offsets - length / 2 + 0.5) / fine_count
    taper = 0.5 - 0.5 * jnp.cos(2.0 * math.pi * (offsets + 0.5) / length)
    window = jnp.sinc(shifted) * taper
    window = window / jnp.sqrt(jnp.sum(window * window))
    return window.reshape(tap_count, fine_count)


def kernels(window, fine_count):
    points = jnp.arange(fine_count)
    phase_steps = points[:, None] * points[None, :] % fine_count
    angles = 2.0 * math.pi * phase_steps.astype(jnp.float32) / fine_count
    cosine = jnp.cos(angles)
    sine_part = jnp.sin(angles)
    result = []
    for tap_index in range(window.shape[0]):
        weights = window[tap_index][:, None]
        hcos = weights * cosine
        hsin = weights * sine_part
        result.append(jnp.stack([jnp.stack([hcos, -hsin]), jnp.stack([hsin, hcos])]))
    return jnp.stack(result)


def packed_rows(left_rows, right_rows, left_all, row_start):
    real_sums = jnp.einsum("cif,cjf->cij", left_rows, left_all, preferred_element_type=jnp.float32)
    imag_sums = jnp.einsum("cif,cjf->cij", right_rows, left_all, preferred_element_type=jnp.float32)
    row_index = row_start + jnp.arange(left_rows.shape[1])
    col_index = jnp.arange(left_all.shape[1])
    upper = row_index[:, None] <= col_index[None, :]
    return jnp.where(upper[None], real_sums, imag_sums)


def local(voltages, gains):
    coarse = voltages.shape[1]
    local_inputs = voltages.shape[2]
    samples = voltages.shape[3]
    frames = samples // FINE
    window = prototype(TAPS, FINE)
    filters = kernels(window, FINE)
    filter_table = jnp.transpose(filters, (1, 0, 3, 2, 4))
    filter_high = filter_table.astype(jnp.bfloat16)
    filter_low = (filter_table - filter_high.astype(jnp.float32)).astype(jnp.bfloat16)
    padded = jnp.pad(voltages, ((0, 0), (0, 0), (0, 0), (0, (TAPS - 1) * FINE)))
    stacked = jnp.stack(
        [padded[..., tap_index * FINE : tap_index * FINE + samples] for tap_index in range(TAPS)],
        axis=1,
    )
    stacked = stacked.reshape(2, TAPS, coarse, local_inputs, frames, FINE)
    spectra = jnp.einsum(
        "atcnmp,atpbk->bcknm", stacked, filter_high, preferred_element_type=jnp.float32
    )
    spectra = spectra + jnp.einsum(
        "atcnmp,atpbk->bcknm", stacked, filter_low, preferred_element_type=jnp.float32
    )
    gain_real = jnp.swapaxes(gains[0], 1, 2)[:, :, :, None]
    gain_imag = jnp.swapaxes(gains[1], 1, 2)[:, :, :, None]
    real_part = spectra[0] * gain_real - spectra[1] * gain_imag
    imag_part = spectra[0] * gain_imag + spectra[1] * gain_real
    outgoing = jnp.stack([real_part, imag_part]).astype(jnp.bfloat16)
    outgoing = outgoing.reshape(2, coarse * FINE, local_inputs, frames)
    turned = lax.all_to_all(outgoing, "inp", split_axis=1, concat_axis=2, tiled=True)
    inputs = turned.shape[2]
    span_count = lax.axis_size("span")
    row_count = inputs // span_count
    frame_scale = 1.0 / (span_count * frames)
    row_start = lax.axis_index("span") * row_count
    frame_piece = lax.all_gather(turned, "span", axis=3, tiled=True)
    left_all = jnp.concatenate([frame_piece[0], frame_piece[1]], axis=-1)
    own_rows = lax.dynamic_slice_in_dim(frame_piece, row_start, row_count, 2)
    left_rows = jnp.concatenate([own_rows[0], own_rows[1]], axis=-1)
    right_rows = jnp.concatenate([own_rows[1], -own_rows[0]], axis=-1)
    summed = packed_rows(left_rows, right_rows, left_all, row_start) * frame_scale
    return summed.astype(jnp.bfloat16)


def order_of(step, mine, coarse):
    if coarse == 4:
        high = (mine // 2 + 1 - step // 2) % 2
        low = (mine % 2 + (step + 1) // 2) % 2
        return 2 * high + low
    return (mine + step + 1) % coarse


def origin_of(step, mine, coarse):
    if coarse == 4:
        return order_of(step, mine, coarse)
    return (mine + coarse - (step + 1) % coarse) % coarse


def filter_rows(fine_count, tap_count, group):
    length = tap_count * fine_count
    offsets = np.arange(length, dtype=np.float64)
    shifted = (offsets - length / 2 + 0.5) / fine_count
    taper = 0.5 - 0.5 * np.cos(2.0 * np.pi * (offsets + 0.5) / length)
    window = np.sinc(shifted) * taper
    window = window / np.sqrt(np.sum(window * window))
    fine = np.arange(fine_count)
    angles = 2.0 * np.pi * ((offsets[None, :] * fine[:, None]) % fine_count) / fine_count
    hcos = window[None, :] * np.cos(angles)
    hsin = window[None, :] * np.sin(angles)
    span = group * fine_count + length
    rows = np.zeros((group, 2, fine_count, 2, span), np.float64)
    for frame in range(group):
        at = slice(frame * fine_count, frame * fine_count + length)
        rows[frame, 0, :, 0, at] = hcos
        rows[frame, 0, :, 1, at] = hsin
        rows[frame, 1, :, 0, at] = -hsin
        rows[frame, 1, :, 1, at] = hcos
    rows = rows.reshape(group * 2 * fine_count, 2 * span).astype(np.float32)
    high = rows.astype(jnp.bfloat16)
    low = (rows - high.astype(np.float32)).astype(jnp.bfloat16)
    return high, low


def products(dims, span, source, turned, result):
    ranks, _, _, local_inputs, frames, _, scale = dims
    rows = ranks * local_inputs // 2
    own_sources = ranks // 2
    depth = 2 * frames
    width = 2 * local_inputs

    def turn_over(part):
        @pl.loop(0, own_sources)
        def _(index):
            at = pl.ds(pl.multiple_of(index * local_inputs, local_inputs), local_inputs)
            where_real = pl.ds(pl.multiple_of(part * frames, frames), frames)
            where_imag = pl.ds(pl.multiple_of(depth + part * frames, frames), frames)
            real = source[part, span * own_sources + index, 0].T
            imag = source[part, span * own_sources + index, 1].T
            turned[0, at, where_real] = real
            turned[0, at, where_imag] = imag
            turned[1, at, where_real] = imag
            turned[1, at, where_imag] = -real

    def columns_of(pair):
        columns = []
        for side in range(2):
            other = pair * 2 + side
            columns.append(
                jnp.concatenate(
                    [source[part, other, piece] for piece in range(2) for part in range(2)], axis=0
                )
            )
        return jnp.concatenate(columns, axis=1)

    def multiply(index):
        @pl.loop(0, ranks // 4)
        def _(step):
            pair = (1 - span) * (ranks // 4) + step
            block = columns_of(pair)
            value = jnp.dot(turned[span], block, preferred_element_type=jnp.float32) * scale
            at = pl.multiple_of(pair * width, width)
            result[index, :, pl.ds(at, width)] = value.astype(jnp.bfloat16)

        @pl.loop(0, ranks // 4)
        def _(step):
            pair = span * (ranks // 4) + step
            block = columns_of(pair)
            real = jnp.dot(turned[0], block, preferred_element_type=jnp.float32)
            imag = jnp.dot(turned[1], block, preferred_element_type=jnp.float32)
            row = lax.broadcasted_iota(jnp.int32, (rows, width), 0)
            column = step * width + lax.broadcasted_iota(jnp.int32, (rows, width), 1)
            value = jnp.where(row <= column, real, imag) * scale
            at = pl.multiple_of(pair * width, width)
            result[index, :, pl.ds(at, width)] = value.astype(jnp.bfloat16)

    return turn_over, multiply


def finish_kernel(dims, done, last, vis, turned, obuf, outsem, osem):
    chunks = dims[2]
    span = lax.axis_index("span")
    turn_over, multiply = products(dims, span, last, turned, obuf)

    def give(channel):
        return pltpu.make_async_copy(done.at[channel], vis.at[channel], outsem.at[channel])

    for channel in range(chunks - 1):
        give(channel).start()
    for part in range(2):
        turn_over(part)
    multiply(0)
    result = pltpu.make_async_copy(obuf.at[0], vis.at[chunks - 1], osem)
    result.start()
    for channel in range(chunks - 1):
        give(channel).wait()
    result.wait()


def fused_kernel(
    dims, volt, gains_in, filters_in, vis, recv, last,
    send, xbuf, tbuf, filters, gains, bbuf, turned,
    xsem, fsem, gsem, ownsem, ssem, lssem, rsem, firstsem, lrsem, psend, precv, plsend, plrecv, bsem,
):
    ranks, coarse, chunks, local_inputs, frames, first, scale = dims
    halves = ranks // coarse
    samples = frames * FINE
    rest = frames - first
    many = chunks - 1
    ahead = min(3, many)
    early_far, early_near = min(3, ahead), min(3, ahead)
    beam = lax.axis_index("beam")
    me = lax.axis_index("inp")
    span = lax.axis_index("span")
    mine = me // halves
    my_half = me % halves
    here = (beam, me, 1 - span)

    def peer(step, turn):
        return order_of(step, mine, coarse) * halves + (my_half + turn) % halves

    def source(step, turn):
        return origin_of(step, mine, coarse) * halves + (my_half + turn) % halves

    peers = [(step, turn) for step in range(coarse) for turn in range(halves)]
    peers = [pair for pair in peers if pair != (coarse - 1, 0)]

    barrier = pltpu.get_barrier_semaphore()
    for step, turn in peers:
        pl.semaphore_signal(barrier, inc=1, device_id=(beam, peer(step, turn), span), device_id_type=MESH)
    pl.semaphore_signal(barrier, inc=1, device_id=here, device_id_type=MESH)

    early = first * FINE + TAPS * FINE

    def load(step, slot, piece=None):
        block = order_of(step, mine, coarse)
        at = pl.ds(0, samples) if piece is None else (pl.ds(0, early), pl.ds(early, samples - early))[piece]
        return pltpu.make_async_copy(
            volt.at[:, block, :, at], xbuf.at[slot, :, :, at], xsem.at[slot if piece is None else 2 * piece]
        )

    load(0, 0, 0).start()
    take_filters = pltpu.make_async_copy(filters_in, filters, fsem)
    take_gains = pltpu.make_async_copy(gains_in, gains, gsem)
    take_filters.start()
    take_gains.start()

    tail = jnp.zeros((2, local_inputs, TAPS * FINE), jnp.bfloat16)
    xbuf[0, :, :, pl.ds(samples, TAPS * FINE)] = tail
    xbuf[1, :, :, pl.ds(samples, TAPS * FINE)] = tail

    def remote(step, turn, src, dst, send_sem, recv_sem):
        return pltpu.make_async_remote_copy(
            src_ref=src, dst_ref=dst, send_sem=send_sem, recv_sem=recv_sem,
            device_id=(beam, peer(step, turn), span), device_id_type=MESH,
        )

    def early_of(step):
        return early_far if 2 * step < coarse else early_near

    def span_of(step):
        return pl.ds(first, rest) if step == 0 else pl.ds(0, frames)

    def outgoing(step, turn, chunk):
        other, at = peer(step, turn), span_of(step)
        return remote(
            step, turn, send.at[other, chunk, :, at], recv.at[span, chunk, me, :, at],
            ssem.at[other], rsem.at[chunk, me],
        )

    def outgoing_last(step, turn, at=None):
        other, at = peer(step, turn), span_of(step) if at is None else at
        return remote(
            step, turn, send.at[other, many, :, at], last.at[span, me, :, at], lssem.at[other], lrsem.at[me]
        )

    def outgoing_first(turn):
        other, at = peer(0, turn), pl.ds(0, first)
        return remote(
            0, turn, send.at[other, pl.ds(0, many), :, at], recv.at[span, :, me, :, at],
            ssem.at[other], firstsem.at[me],
        )

    def sent(step, turn):
        other = peer(step, turn)
        return remote(
            step, turn, send.at[other, pl.ds(0, many)], recv.at[span, :, me], ssem.at[other], firstsem.at[me]
        )

    def incoming(step, turn, chunk):
        other, at = source(step, turn), span_of(step)
        return remote(
            step, turn, recv.at[span, chunk, other, :, at], recv.at[span, chunk, other, :, at],
            ssem.at[other], rsem.at[chunk, other],
        )

    def incoming_first(turn):
        other, at = source(0, turn), pl.ds(0, first)
        return remote(
            0, turn, recv.at[span, :, other, :, at], recv.at[span, :, other, :, at],
            ssem.at[other], firstsem.at[other],
        )

    def incoming_last(other):
        return remote(0, 0, last.at[span, other], last.at[span, other], lssem.at[other], lrsem.at[other])

    def across(ref, send_sem, recv_sem):
        return pltpu.make_async_remote_copy(
            src_ref=ref, dst_ref=ref, send_sem=send_sem, recv_sem=recv_sem,
            device_id=here, device_id_type=MESH,
        )

    def channelize(slot, start, count):
        @pl.loop(0, count // 8, unroll=2)
        def _(pair):
            base = pl.multiple_of(start * FINE + pair * (8 * FINE), 4 * FINE)
            pieces = []
            for part in range(2):
                at = base + part * 4 * FINE
                at = pl.multiple_of(at, 4 * FINE)
                pieces.append(
                    jnp.concatenate(
                        [xbuf[slot, 0, :, pl.ds(at, 8 * FINE)], xbuf[slot, 1, :, pl.ds(at, 8 * FINE)]],
                        axis=1,
                    )
                )
            both = jnp.concatenate(pieces, axis=0)
            contract = (((1,), (1,)), ((), ()))
            got = lax.dot_general(filters[0], both, contract, preferred_element_type=jnp.float32)
            got = got + lax.dot_general(filters[1], both, contract, preferred_element_type=jnp.float32)
            at = pl.multiple_of(pair * (16 * FINE), 16 * FINE)
            tbuf[pl.ds(at, 8 * FINE), :] = got[:, :local_inputs]
            tbuf[pl.ds(at + 8 * FINE, 8 * FINE), :] = got[:, local_inputs:]

    def weigh(step, turn, start, count):
        block = order_of(step, mine, coarse)
        half = (my_half + turn) % halves
        other = peer(step, turn)

        @pl.loop(0, chunks, unroll=2)
        def _(chunk):
            fine = half * chunks + chunk
            real = tbuf[pl.ds(fine, count, stride=2 * FINE), :]
            imag = tbuf[pl.ds(FINE + fine, count, stride=2 * FINE), :]
            gain_real = gains[0, block, pl.ds(fine, 1), :]
            gain_imag = gains[1, block, pl.ds(fine, 1), :]
            at = pl.ds(start, count)
            send[other, chunk, 0, at] = (real * gain_real - imag * gain_imag).astype(jnp.bfloat16)
            send[other, chunk, 1, at] = (real * gain_imag + imag * gain_real).astype(jnp.bfloat16)

    load(0, 0, 0).wait()
    take_filters.wait()
    load(0, 0, 1).start()
    load(1, 1).start()
    channelize(0, 0, first)
    take_gains.wait()
    for turn in range(halves):
        weigh(0, turn, 0, first)
        if turn == 0:
            pl.semaphore_wait(barrier, len(peers) + 1)
        if (0, turn) in peers:
            outgoing_first(turn).start()
            outgoing_last(0, turn, pl.ds(0, first)).start()
    for step in range(coarse):
        slot = step % 2
        start = first if step == 0 else 0
        if step == 0:
            load(0, 0, 1).wait()
        else:
            load(step, slot).wait()
        channelize(slot, start, frames - start)
        if step + 2 < coarse:
            load(step + 2, slot).start()
        for turn in range(halves):
            weigh(step, turn, start, frames - start)
            if (step, turn) in peers:

                for chunk in range(early_of(step)):
                    outgoing(step, turn, chunk).start()
            else:
                own = pltpu.make_async_copy(send.at[me, pl.ds(0, many)], recv.at[span, :, me], ownsem.at[0])
                own_last = pltpu.make_async_copy(send.at[me, many], last.at[span, me], ownsem.at[1])
                own.start()
                own_last.start()
    for chunk in range(ahead):
        for step, turn in peers:
            if chunk >= early_of(step):
                outgoing(step, turn, chunk).start()
    own.wait()
    own_last.wait()

    for turn in range(halves):
        if (0, turn) in peers:
            incoming_first(turn).wait_recv()

    def forward(chunk):
        return across(recv.at[span, chunk], psend.at[0], precv.at[chunk])

    def backward(chunk):
        return across(recv.at[1 - span, chunk], psend.at[0], precv.at[chunk])

    def fetch(chunk, part):
        return pltpu.make_async_copy(recv.at[part, chunk], bbuf.at[part], bsem.at[part])

    turn_over, multiply = products(dims, span, bbuf, turned, vis)

    @pl.loop(0, many)
    def _(chunk):
        for step, turn in peers:
            incoming(step, turn, chunk).wait_recv()
        forward(chunk).start()

        @pl.when(chunk + ahead < many)
        def _():
            for step, turn in peers:
                outgoing(step, turn, chunk + ahead).start()

        @pl.when(chunk + ahead == many)
        def _():
            for step, turn in peers:
                outgoing_last(step, turn).start()

        fetch(chunk, span).start()
        fetch(chunk, span).wait()
        turn_over(span)
        backward(chunk).wait_recv()
        fetch(chunk, 1 - span).start()
        fetch(chunk, 1 - span).wait()
        turn_over(1 - span)
        multiply(chunk)

    def forward_last(other):
        return across(last.at[span, other], plsend.at[other], plrecv.at[other])

    def backward_last(other):
        return across(last.at[1 - span, other], plsend.at[other], plrecv.at[other])

    inner = (mine // 2 + mine % 2) % 2
    pairs = [(source(0, turn), source(1, turn)) for turn in range(halves)]
    final = [source(step, turn) for step, turn in peers if step > 1]
    final += [inner * one + (1 - inner) * other for one, other in pairs]
    final += [(1 - inner) * one + inner * other for one, other in pairs]
    forward_last(me).start()
    for other in final:
        incoming_last(other).wait_recv()
        forward_last(other).start()
    for step, turn in peers:
        sent(step, turn).wait_send()
        outgoing_last(step, turn, pl.ds(0, frames)).wait_send()
    across(recv.at[span], psend.at[0], precv.at[0]).wait_send()
    for other in [me] + final:
        forward_last(other).wait_send()
        backward_last(other).wait_recv()


def fused(voltages, gains):
    coarse, local_inputs, samples = voltages.shape[1:]
    ranks = lax.axis_size("inp")
    frames = samples // FINE
    halves = ranks // coarse
    chunks = FINE // halves
    rows = ranks * local_inputs // 2
    columns = ranks * local_inputs
    first = 32
    filters = jnp.asarray(np.stack(filter_rows(FINE, TAPS, 4)))
    gain_rows = jnp.swapaxes(gains, 2, 3)
    scale = 1.0 / (2 * frames)
    dims = (ranks, coarse, chunks, local_inputs, frames, first, scale)
    bf16 = jnp.bfloat16
    anywhere = pl.BlockSpec(memory_space=pl.ANY)
    inside = pl.BlockSpec(memory_space=pltpu.VMEM)
    flops = 4 * chunks * rows * columns * 4 * frames
    done, _, last = pl.pallas_call(
        functools.partial(fused_kernel, dims),
        out_shape=(
            pltpu.VMEM((chunks - 1, rows, columns), bf16),
            jax.ShapeDtypeStruct((2, chunks - 1, ranks, 2, frames, local_inputs), bf16),
            pltpu.VMEM((2, ranks, 2, frames, local_inputs), bf16),
        ),
        in_specs=[anywhere, anywhere, anywhere],
        out_specs=(inside, anywhere, inside),
        scratch_shapes=[
            pltpu.VMEM((ranks, chunks, 2, frames, local_inputs), bf16),
            pltpu.VMEM((2, 2, local_inputs, samples + TAPS * FINE), bf16),
            pltpu.VMEM((frames * 2 * FINE, local_inputs), jnp.float32),
            pltpu.VMEM(filters.shape, bf16),
            pltpu.VMEM(gain_rows.shape, jnp.float32),
            pltpu.VMEM((2, ranks, 2, frames, local_inputs), bf16),
            pltpu.VMEM((2, rows, 4 * frames), bf16),
            pltpu.SemaphoreType.DMA((3,)),
            pltpu.SemaphoreType.DMA,
            pltpu.SemaphoreType.DMA,
            pltpu.SemaphoreType.DMA((2,)),
            pltpu.SemaphoreType.DMA((ranks,)),
            pltpu.SemaphoreType.DMA((ranks,)),
            pltpu.SemaphoreType.DMA((chunks - 1, ranks)),
            pltpu.SemaphoreType.DMA((ranks,)),
            pltpu.SemaphoreType.DMA((ranks,)),
            pltpu.SemaphoreType.DMA((1,)),
            pltpu.SemaphoreType.DMA((chunks - 1,)),
            pltpu.SemaphoreType.DMA((ranks,)),
            pltpu.SemaphoreType.DMA((ranks,)),
            pltpu.SemaphoreType.DMA((2,)),
        ],
        compiler_params=pltpu.CompilerParams(
            collective_id=0, has_side_effects=True, vmem_limit_bytes=44 * 1024 * 1024
        ),
        cost_estimate=pl.CostEstimate(flops=flops, bytes_accessed=2 * voltages.size * 8, transcendentals=0),
    )(voltages, gain_rows, filters)
    done = pltpu.with_memory_space_constraint(done, pltpu.VMEM)
    last = pltpu.with_memory_space_constraint(last, pltpu.VMEM)
    return pl.pallas_call(
        functools.partial(finish_kernel, dims),
        out_shape=jax.ShapeDtypeStruct((chunks, rows, columns), bf16),
        in_specs=[inside, inside],
        out_specs=anywhere,
        scratch_shapes=[
            pltpu.VMEM((2, rows, 4 * frames), bf16),
            pltpu.VMEM((1, rows, columns), bf16),
            pltpu.SemaphoreType.DMA((chunks - 1,)),
            pltpu.SemaphoreType.DMA,
        ],
        compiler_params=pltpu.CompilerParams(vmem_limit_bytes=24 * 1024 * 1024),
    )(done, last)


def vmem_needed(coarse, local_inputs, samples, ranks):
    frames = samples // FINE
    chunks = FINE * coarse // ranks
    spectra = 4 * frames * local_inputs
    columns = ranks * local_inputs
    kept = chunks * columns * columns + 2 * ranks * spectra
    sending = ranks * chunks * spectra
    sampled = 8 * local_inputs * (samples + TAPS * FINE)
    channelized = frames * 2 * FINE * local_inputs * 4
    correlated = 2 * ranks * spectra + columns * 4 * frames * 2
    return kept, sending + sampled + channelized + correlated


def chosen(voltages, gains):
    coarse, local_inputs, samples = voltages.shape[1:]
    ranks, spans = lax.axis_size("inp"), lax.axis_size("span")
    fits = (
        spans == 2
        and local_inputs % 128 == 0
        and coarse > 2
        and ranks % coarse == 0
        and ranks % 4 == 0
        and FINE % (ranks // coarse) == 0
        and samples % (16 * FINE) == 0
        and samples >= 64 * FINE
    )
    if fits:
        kept, working = vmem_needed(coarse, local_inputs, samples, ranks)
        fits = kept <= 18 * 1024 * 1024 and working <= 42 * 1024 * 1024
    return fused(voltages, gains) if fits else local(voltages, gains)


def solution(mesh):
    placed = (P(None, "beam", "inp", "span"), P(None, "beam", "inp", None))
    return jax.shard_map(
        chosen,
        mesh=mesh,
        in_specs=placed,
        out_specs=P(("beam", "inp"), "span", None),
        check_vma=False,
    )
```

```python
import functools
import math

import jax
import jax.numpy as jnp
import numpy as np
from jax import lax
from jax.experimental import pallas as pl
from jax.experimental.pallas import tpu as pltpu
from jax.sharding import PartitionSpec as P

FINE = 32
TAPS = 4
MESH = pl.DeviceIdType.MESH


def prototype(tap_count, fine_count):
    length = tap_count * fine_count
    offsets = jnp.arange(length).astype(jnp.float32)
    shifted = (offsets - length / 2 + 0.5) / fine_count
    taper = 0.5 - 0.5 * jnp.cos(2.0 * math.pi * (offsets + 0.5) / length)
    window = jnp.sinc(shifted) * taper
    window = window / jnp.sqrt(jnp.sum(window * window))
    return window.reshape(tap_count, fine_count)


def kernels(window, fine_count):
    points = jnp.arange(fine_count)
    phase_steps = points[:, None] * points[None, :] % fine_count
    angles = 2.0 * math.pi * phase_steps.astype(jnp.float32) / fine_count
    cosine = jnp.cos(angles)
    sine_part = jnp.sin(angles)
    result = []
    for tap_index in range(window.shape[0]):
        weights = window[tap_index][:, None]
        hcos = weights * cosine
        hsin = weights * sine_part
        result.append(jnp.stack([jnp.stack([hcos, -hsin]), jnp.stack([hsin, hcos])]))
    return jnp.stack(result)


def packed_rows(left_rows, right_rows, left_all, row_start):
    real_sums = jnp.einsum("cif,cjf->cij", left_rows, left_all, preferred_element_type=jnp.float32)
    imag_sums = jnp.einsum("cif,cjf->cij", right_rows, left_all, preferred_element_type=jnp.float32)
    row_index = row_start + jnp.arange(left_rows.shape[1])
    col_index = jnp.arange(left_all.shape[1])
    upper = row_index[:, None] <= col_index[None, :]
    return jnp.where(upper[None], real_sums, imag_sums)


def local(voltages, gains):
    coarse = voltages.shape[1]
    local_inputs = voltages.shape[2]
    samples = voltages.shape[3]
    frames = samples // FINE
    window = prototype(TAPS, FINE)
    filters = kernels(window, FINE)
    filter_table = jnp.transpose(filters, (1, 0, 3, 2, 4))
    filter_high = filter_table.astype(jnp.bfloat16)
    filter_low = (filter_table - filter_high.astype(jnp.float32)).astype(jnp.bfloat16)
    padded = jnp.pad(voltages, ((0, 0), (0, 0), (0, 0), (0, (TAPS - 1) * FINE)))
    stacked = jnp.stack(
        [padded[..., tap_index * FINE : tap_index * FINE + samples] for tap_index in range(TAPS)],
        axis=1,
    )
    stacked = stacked.reshape(2, TAPS, coarse, local_inputs, frames, FINE)
    spectra = jnp.einsum(
        "atcnmp,atpbk->bcknm", stacked, filter_high, preferred_element_type=jnp.float32
    )
    spectra = spectra + jnp.einsum(
        "atcnmp,atpbk->bcknm", stacked, filter_low, preferred_element_type=jnp.float32
    )
    gain_real = jnp.swapaxes(gains[0], 1, 2)[:, :, :, None]
    gain_imag = jnp.swapaxes(gains[1], 1, 2)[:, :, :, None]
    real_part = spectra[0] * gain_real - spectra[1] * gain_imag
    imag_part = spectra[0] * gain_imag + spectra[1] * gain_real
    outgoing = jnp.stack([real_part, imag_part]).astype(jnp.bfloat16)
    outgoing = outgoing.reshape(2, coarse * FINE, local_inputs, frames)
    turned = lax.all_to_all(outgoing, "inp", split_axis=1, concat_axis=2, tiled=True)
    inputs = turned.shape[2]
    span_count = lax.axis_size("span")
    row_count = inputs // span_count
    frame_scale = 1.0 / (span_count * frames)
    row_start = lax.axis_index("span") * row_count
    frame_piece = lax.all_gather(turned, "span", axis=3, tiled=True)
    left_all = jnp.concatenate([frame_piece[0], frame_piece[1]], axis=-1)
    own_rows = lax.dynamic_slice_in_dim(frame_piece, row_start, row_count, 2)
    left_rows = jnp.concatenate([own_rows[0], own_rows[1]], axis=-1)
    right_rows = jnp.concatenate([own_rows[1], -own_rows[0]], axis=-1)
    summed = packed_rows(left_rows, right_rows, left_all, row_start) * frame_scale
    return summed.astype(jnp.bfloat16)


def order_of(step, mine, coarse):
    if coarse == 4:
        high = (mine // 2 + 1 - step // 2) % 2
        low = (mine % 2 + (step + 1) // 2) % 2
        return 2 * high + low
    return (mine + step + 1) % coarse


def origin_of(step, mine, coarse):
    if coarse == 4:
        return order_of(step, mine, coarse)
    return (mine + coarse - (step + 1) % coarse) % coarse


def filter_rows(fine_count, tap_count, group):
    length = tap_count * fine_count
    offsets = np.arange(length, dtype=np.float64)
    shifted = (offsets - length / 2 + 0.5) / fine_count
    taper = 0.5 - 0.5 * np.cos(2.0 * np.pi * (offsets + 0.5) / length)
    window = np.sinc(shifted) * taper
    window = window / np.sqrt(np.sum(window * window))
    fine = np.arange(fine_count)
    angles = 2.0 * np.pi * ((offsets[None, :] * fine[:, None]) % fine_count) / fine_count
    hcos = window[None, :] * np.cos(angles)
    hsin = window[None, :] * np.sin(angles)
    span = group * fine_count + length
    rows = np.zeros((group, 2, fine_count, 2, span), np.float64)
    for frame in range(group):
        at = slice(frame * fine_count, frame * fine_count + length)
        rows[frame, 0, :, 0, at] = hcos
        rows[frame, 0, :, 1, at] = hsin
        rows[frame, 1, :, 0, at] = -hsin
        rows[frame, 1, :, 1, at] = hcos
    rows = rows.reshape(group * 2 * fine_count, 2 * span).astype(np.float32)
    high = rows.astype(jnp.bfloat16)
    low = (rows - high.astype(np.float32)).astype(jnp.bfloat16)
    return high, low


def products(dims, span, source, turned, result):
    ranks, _, _, local_inputs, frames, _, scale = dims
    rows = ranks * local_inputs // 2
    own_sources = ranks // 2
    depth = 2 * frames
    width = 2 * local_inputs

    def turn_over(part):
        @pl.loop(0, own_sources)
        def _(index):
            at = pl.ds(pl.multiple_of(index * local_inputs, local_inputs), local_inputs)
            where_real = pl.ds(pl.multiple_of(part * frames, frames), frames)
            where_imag = pl.ds(pl.multiple_of(depth + part * frames, frames), frames)
            real = source[part, span * own_sources + index, 0].T
            imag = source[part, span * own_sources + index, 1].T
            turned[0, at, where_real] = real
            turned[0, at, where_imag] = imag
            turned[1, at, where_real] = imag
            turned[1, at, where_imag] = -real

    def columns_of(pair):
        columns = []
        for side in range(2):
            other = pair * 2 + side
            columns.append(
                jnp.concatenate(
                    [source[part, other, piece] for piece in range(2) for part in range(2)], axis=0
                )
            )
        return jnp.concatenate(columns, axis=1)

    def multiply(index):
        @pl.loop(0, ranks // 4)
        def _(step):
            pair = (1 - span) * (ranks // 4) + step
            block = columns_of(pair)
            value = jnp.dot(turned[span], block, preferred_element_type=jnp.float32) * scale
            at = pl.multiple_of(pair * width, width)
            result[index, :, pl.ds(at, width)] = value.astype(jnp.bfloat16)

        @pl.loop(0, ranks // 4)
        def _(step):
            pair = span * (ranks // 4) + step
            block = columns_of(pair)
            real = jnp.dot(turned[0], block, preferred_element_type=jnp.float32)
            imag = jnp.dot(turned[1], block, preferred_element_type=jnp.float32)
            row = lax.broadcasted_iota(jnp.int32, (rows, width), 0)
            column = step * width + lax.broadcasted_iota(jnp.int32, (rows, width), 1)
            value = jnp.where(row <= column, real, imag) * scale
            at = pl.multiple_of(pair * width, width)
            result[index, :, pl.ds(at, width)] = value.astype(jnp.bfloat16)

    return turn_over, multiply


def finish_kernel(dims, done, last, vis, turned, obuf, outsem, osem):
    chunks = dims[2]
    span = lax.axis_index("span")
    turn_over, multiply = products(dims, span, last, turned, obuf)

    def give(channel):
        return pltpu.make_async_copy(done.at[channel], vis.at[channel], outsem.at[channel])

    for channel in range(chunks - 1):
        give(channel).start()
    for part in range(2):
        turn_over(part)
    multiply(0)
    result = pltpu.make_async_copy(obuf.at[0], vis.at[chunks - 1], osem)
    result.start()
    for channel in range(chunks - 1):
        give(channel).wait()
    result.wait()


def fused_kernel(
    dims, volt, gains_in, filters_in, vis, recv, last,
    send, xbuf, tbuf, filters, gains, bbuf, turned,
    xsem, fsem, gsem, ownsem, ssem, lssem, rsem, firstsem, lrsem, psend, precv, plsend, plrecv, bsem,
):
    ranks, coarse, chunks, local_inputs, frames, first, scale = dims
    halves = ranks // coarse
    samples = frames * FINE
    rest = frames - first
    many = chunks - 1
    ahead = min(3, many)
    early_far, early_near = min(3, ahead), min(3, ahead)
    beam = lax.axis_index("beam")
    me = lax.axis_index("inp")
    span = lax.axis_index("span")
    mine = me // halves
    my_half = me % halves
    here = (beam, me, 1 - span)

    def peer(step, turn):
        return order_of(step, mine, coarse) * halves + (my_half + turn) % halves

    def source(step, turn):
        return origin_of(step, mine, coarse) * halves + (my_half + turn) % halves

    peers = [(step, turn) for step in range(coarse) for turn in range(halves)]
    peers = [pair for pair in peers if pair != (coarse - 1, 0)]

    early = first * FINE + TAPS * FINE

    def load(step, slot, piece=None):
        block = order_of(step, mine, coarse)
        at = pl.ds(0, samples) if piece is None else (pl.ds(0, early), pl.ds(early, samples - early))[piece]
        return pltpu.make_async_copy(
            volt.at[:, block, :, at], xbuf.at[slot, :, :, at], xsem.at[slot if piece is None else 2 * piece]
        )

    load(0, 0, 0).start()
    take_filters = pltpu.make_async_copy(filters_in, filters, fsem)
    take_gains = pltpu.make_async_copy(gains_in, gains, gsem)
    take_filters.start()
    take_gains.start()

    barrier = pltpu.get_barrier_semaphore()
    for step, turn in peers:
        pl.semaphore_signal(barrier, inc=1, device_id=(beam, peer(step, turn), span), device_id_type=MESH)
    pl.semaphore_signal(barrier, inc=1, device_id=here, device_id_type=MESH)


    tail = jnp.zeros((2, local_inputs, TAPS * FINE), jnp.bfloat16)
    xbuf[0, :, :, pl.ds(samples, TAPS * FINE)] = tail
    xbuf[1, :, :, pl.ds(samples, TAPS * FINE)] = tail

    def remote(step, turn, src, dst, send_sem, recv_sem):
        return pltpu.make_async_remote_copy(
            src_ref=src, dst_ref=dst, send_sem=send_sem, recv_sem=recv_sem,
            device_id=(beam, peer(step, turn), span), device_id_type=MESH,
        )

    def early_of(step):
        return early_far if 2 * step < coarse else early_near

    def span_of(step):
        return pl.ds(first, rest) if step == 0 else pl.ds(0, frames)

    def outgoing(step, turn, chunk):
        other, at = peer(step, turn), span_of(step)
        return remote(
            step, turn, send.at[other, chunk, :, at], recv.at[span, chunk, me, :, at],
            ssem.at[other], rsem.at[chunk, me],
        )

    def outgoing_last(step, turn, at=None):
        other, at = peer(step, turn), span_of(step) if at is None else at
        return remote(
            step, turn, send.at[other, many, :, at], last.at[span, me, :, at], lssem.at[other], lrsem.at[me]
        )

    def outgoing_first(turn, at):
        other = peer(0, turn)
        return remote(
            0, turn, send.at[other, pl.ds(0, many), :, at], recv.at[span, :, me, :, at],
            ssem.at[other], firstsem.at[me],
        )

    def sent(step, turn):
        other = peer(step, turn)
        return remote(
            step, turn, send.at[other, pl.ds(0, many)], recv.at[span, :, me], ssem.at[other], firstsem.at[me]
        )

    def incoming(step, turn, chunk):
        other, at = source(step, turn), span_of(step)
        return remote(
            step, turn, recv.at[span, chunk, other, :, at], recv.at[span, chunk, other, :, at],
            ssem.at[other], rsem.at[chunk, other],
        )

    def incoming_first(turn):
        other, at = source(0, turn), pl.ds(0, first)
        return remote(
            0, turn, recv.at[span, :, other, :, at], recv.at[span, :, other, :, at],
            ssem.at[other], firstsem.at[other],
        )

    def incoming_last(other):
        return remote(0, 0, last.at[span, other], last.at[span, other], lssem.at[other], lrsem.at[other])

    def across(ref, send_sem, recv_sem):
        return pltpu.make_async_remote_copy(
            src_ref=ref, dst_ref=ref, send_sem=send_sem, recv_sem=recv_sem,
            device_id=here, device_id_type=MESH,
        )

    def channelize(slot, start, count):
        @pl.loop(0, count // 8, unroll=2)
        def _(pair):
            base = pl.multiple_of(start * FINE + pair * (8 * FINE), 4 * FINE)
            pieces = []
            for part in range(2):
                at = base + part * 4 * FINE
                at = pl.multiple_of(at, 4 * FINE)
                pieces.append(
                    jnp.concatenate(
                        [xbuf[slot, 0, :, pl.ds(at, 8 * FINE)], xbuf[slot, 1, :, pl.ds(at, 8 * FINE)]],
                        axis=1,
                    )
                )
            both = jnp.concatenate(pieces, axis=0)
            contract = (((1,), (1,)), ((), ()))
            got = lax.dot_general(filters[0], both, contract, preferred_element_type=jnp.float32)
            got = got + lax.dot_general(filters[1], both, contract, preferred_element_type=jnp.float32)
            at = pl.multiple_of(pair * (16 * FINE), 16 * FINE)
            tbuf[pl.ds(at, 8 * FINE), :] = got[:, :local_inputs]
            tbuf[pl.ds(at + 8 * FINE, 8 * FINE), :] = got[:, local_inputs:]

    def weigh(step, turn, start, count):
        block = order_of(step, mine, coarse)
        half = (my_half + turn) % halves
        other = peer(step, turn)

        @pl.loop(0, chunks, unroll=2)
        def _(chunk):
            fine = half * chunks + chunk
            real = tbuf[pl.ds(fine, count, stride=2 * FINE), :]
            imag = tbuf[pl.ds(FINE + fine, count, stride=2 * FINE), :]
            gain_real = gains[0, block, pl.ds(fine, 1), :]
            gain_imag = gains[1, block, pl.ds(fine, 1), :]
            at = pl.ds(start, count)
            send[other, chunk, 0, at] = (real * gain_real - imag * gain_imag).astype(jnp.bfloat16)
            send[other, chunk, 1, at] = (real * gain_imag + imag * gain_real).astype(jnp.bfloat16)

    load(0, 0, 0).wait()
    take_filters.wait()
    load(0, 0, 1).start()
    load(1, 1).start()
    for begin in range(0, first, first // 2):
        channelize(0, begin, first // 2)
        if begin == 0:
            take_gains.wait()
        for turn in range(halves):
            weigh(0, turn, begin, first // 2)
            if (begin, turn) == (0, 0):
                pl.semaphore_wait(barrier, len(peers) + 1)
            if (0, turn) in peers:
                at = pl.ds(begin, first // 2)
                outgoing_first(turn, at).start()
                outgoing_last(0, turn, at).start()
    for step in range(coarse):
        slot = step % 2
        start = first if step == 0 else 0
        if step == 0:
            load(0, 0, 1).wait()
        else:
            load(step, slot).wait()
        channelize(slot, start, frames - start)
        if step + 2 < coarse:
            load(step + 2, slot).start()
        for turn in range(halves):
            weigh(step, turn, start, frames - start)
            if (step, turn) in peers:

                for chunk in range(early_of(step)):
                    outgoing(step, turn, chunk).start()
            else:
                own = pltpu.make_async_copy(send.at[me, pl.ds(0, many)], recv.at[span, :, me], ownsem.at[0])
                own_last = pltpu.make_async_copy(send.at[me, many], last.at[span, me], ownsem.at[1])
                own.start()
                own_last.start()
    for chunk in range(ahead):
        for step, turn in peers:
            if chunk >= early_of(step):
                outgoing(step, turn, chunk).start()
    own.wait()
    own_last.wait()

    for turn in range(halves):
        if (0, turn) in peers:
            incoming_first(turn).wait_recv()

    def forward(chunk):
        return across(recv.at[span, chunk], psend.at[0], precv.at[chunk])

    def backward(chunk):
        return across(recv.at[1 - span, chunk], psend.at[0], precv.at[chunk])

    def fetch(chunk, part):
        return pltpu.make_async_copy(recv.at[part, chunk], bbuf.at[part], bsem.at[part])

    turn_over, multiply = products(dims, span, bbuf, turned, vis)

    @pl.loop(0, many)
    def _(chunk):
        for step, turn in peers:
            incoming(step, turn, chunk).wait_recv()
        forward(chunk).start()

        @pl.when(chunk + ahead < many)
        def _():
            for step, turn in peers:
                outgoing(step, turn, chunk + ahead).start()

        @pl.when(chunk + ahead == many)
        def _():
            for step, turn in peers:
                outgoing_last(step, turn).start()

        fetch(chunk, span).start()
        fetch(chunk, span).wait()
        turn_over(span)
        backward(chunk).wait_recv()
        fetch(chunk, 1 - span).start()
        fetch(chunk, 1 - span).wait()
        turn_over(1 - span)
        multiply(chunk)

    def forward_last(other):
        return across(last.at[span, other], plsend.at[other], plrecv.at[other])

    def backward_last(other):
        return across(last.at[1 - span, other], plsend.at[other], plrecv.at[other])

    inner = (mine // 2 + mine % 2) % 2
    pairs = [(source(0, turn), source(1, turn)) for turn in range(halves)]
    final = [source(step, turn) for step, turn in peers if step > 1]
    final += [inner * one + (1 - inner) * other for one, other in pairs]
    final += [(1 - inner) * one + inner * other for one, other in pairs]
    forward_last(me).start()
    for other in final:
        incoming_last(other).wait_recv()
        forward_last(other).start()
    for step, turn in peers:
        sent(step, turn).wait_send()
        outgoing_last(step, turn, pl.ds(0, frames)).wait_send()
    across(recv.at[span], psend.at[0], precv.at[0]).wait_send()
    for other in [me] + final:
        forward_last(other).wait_send()
        backward_last(other).wait_recv()


def fused(voltages, gains):
    coarse, local_inputs, samples = voltages.shape[1:]
    ranks = lax.axis_size("inp")
    frames = samples // FINE
    halves = ranks // coarse
    chunks = FINE // halves
    rows = ranks * local_inputs // 2
    columns = ranks * local_inputs
    first = 32
    filters = jnp.asarray(np.stack(filter_rows(FINE, TAPS, 4)))
    gain_rows = jnp.swapaxes(gains, 2, 3)
    scale = 1.0 / (2 * frames)
    dims = (ranks, coarse, chunks, local_inputs, frames, first, scale)
    bf16 = jnp.bfloat16
    anywhere = pl.BlockSpec(memory_space=pl.ANY)
    inside = pl.BlockSpec(memory_space=pltpu.VMEM)
    flops = 4 * chunks * rows * columns * 4 * frames
    done, _, last = pl.pallas_call(
        functools.partial(fused_kernel, dims),
        out_shape=(
            pltpu.VMEM((chunks - 1, rows, columns), bf16),
            jax.ShapeDtypeStruct((2, chunks - 1, ranks, 2, frames, local_inputs), bf16),
            pltpu.VMEM((2, ranks, 2, frames, local_inputs), bf16),
        ),
        in_specs=[anywhere, anywhere, anywhere],
        out_specs=(inside, anywhere, inside),
        scratch_shapes=[
            pltpu.VMEM((ranks, chunks, 2, frames, local_inputs), bf16),
            pltpu.VMEM((2, 2, local_inputs, samples + TAPS * FINE), bf16),
            pltpu.VMEM((frames * 2 * FINE, local_inputs), jnp.float32),
            pltpu.VMEM(filters.shape, bf16),
            pltpu.VMEM(gain_rows.shape, jnp.float32),
            pltpu.VMEM((2, ranks, 2, frames, local_inputs), bf16),
            pltpu.VMEM((2, rows, 4 * frames), bf16),
            pltpu.SemaphoreType.DMA((3,)),
            pltpu.SemaphoreType.DMA,
            pltpu.SemaphoreType.DMA,
            pltpu.SemaphoreType.DMA((2,)),
            pltpu.SemaphoreType.DMA((ranks,)),
            pltpu.SemaphoreType.DMA((ranks,)),
            pltpu.SemaphoreType.DMA((chunks - 1, ranks)),
            pltpu.SemaphoreType.DMA((ranks,)),
            pltpu.SemaphoreType.DMA((ranks,)),
            pltpu.SemaphoreType.DMA((1,)),
            pltpu.SemaphoreType.DMA((chunks - 1,)),
            pltpu.SemaphoreType.DMA((ranks,)),
            pltpu.SemaphoreType.DMA((ranks,)),
            pltpu.SemaphoreType.DMA((2,)),
        ],
        compiler_params=pltpu.CompilerParams(
            collective_id=0, has_side_effects=True, vmem_limit_bytes=44 * 1024 * 1024
        ),
        cost_estimate=pl.CostEstimate(flops=flops, bytes_accessed=2 * voltages.size * 8, transcendentals=0),
    )(voltages, gain_rows, filters)
    done = pltpu.with_memory_space_constraint(done, pltpu.VMEM)
    last = pltpu.with_memory_space_constraint(last, pltpu.VMEM)
    return pl.pallas_call(
        functools.partial(finish_kernel, dims),
        out_shape=jax.ShapeDtypeStruct((chunks, rows, columns), bf16),
        in_specs=[inside, inside],
        out_specs=anywhere,
        scratch_shapes=[
            pltpu.VMEM((2, rows, 4 * frames), bf16),
            pltpu.VMEM((1, rows, columns), bf16),
            pltpu.SemaphoreType.DMA((chunks - 1,)),
            pltpu.SemaphoreType.DMA,
        ],
        compiler_params=pltpu.CompilerParams(vmem_limit_bytes=24 * 1024 * 1024),
    )(done, last)


def vmem_needed(coarse, local_inputs, samples, ranks):
    frames = samples // FINE
    chunks = FINE * coarse // ranks
    spectra = 4 * frames * local_inputs
    columns = ranks * local_inputs
    kept = chunks * columns * columns + 2 * ranks * spectra
    sending = ranks * chunks * spectra
    sampled = 8 * local_inputs * (samples + TAPS * FINE)
    channelized = frames * 2 * FINE * local_inputs * 4
    correlated = 2 * ranks * spectra + columns * 4 * frames * 2
    return kept, sending + sampled + channelized + correlated


def chosen(voltages, gains):
    coarse, local_inputs, samples = voltages.shape[1:]
    ranks, spans = lax.axis_size("inp"), lax.axis_size("span")
    fits = (
        spans == 2
        and local_inputs % 128 == 0
        and coarse > 2
        and ranks % coarse == 0
        and ranks % 4 == 0
        and FINE % (ranks // coarse) == 0
        and samples % (16 * FINE) == 0
        and samples >= 64 * FINE
    )
    if fits:
        kept, working = vmem_needed(coarse, local_inputs, samples, ranks)
        fits = kept <= 18 * 1024 * 1024 and working <= 42 * 1024 * 1024
    return fused(voltages, gains) if fits else local(voltages, gains)


def solution(mesh):
    placed = (P(None, "beam", "inp", "span"), P(None, "beam", "inp", None))
    return jax.shard_map(
        chosen,
        mesh=mesh,
        in_specs=placed,
        out_specs=P(("beam", "inp"), "span", None),
        check_vma=False,
    )
```

```python
import functools
import math

import jax
import jax.numpy as jnp
import numpy as np
from jax import lax
from jax.experimental import pallas as pl
from jax.experimental.pallas import tpu as pltpu
from jax.sharding import PartitionSpec as P

FINE = 32
TAPS = 4
MESH = pl.DeviceIdType.MESH


def prototype(tap_count, fine_count):
    length = tap_count * fine_count
    offsets = jnp.arange(length).astype(jnp.float32)
    shifted = (offsets - length / 2 + 0.5) / fine_count
    taper = 0.5 - 0.5 * jnp.cos(2.0 * math.pi * (offsets + 0.5) / length)
    window = jnp.sinc(shifted) * taper
    window = window / jnp.sqrt(jnp.sum(window * window))
    return window.reshape(tap_count, fine_count)


def kernels(window, fine_count):
    points = jnp.arange(fine_count)
    phase_steps = points[:, None] * points[None, :] % fine_count
    angles = 2.0 * math.pi * phase_steps.astype(jnp.float32) / fine_count
    cosine = jnp.cos(angles)
    sine_part = jnp.sin(angles)
    result = []
    for tap_index in range(window.shape[0]):
        weights = window[tap_index][:, None]
        hcos = weights * cosine
        hsin = weights * sine_part
        result.append(jnp.stack([jnp.stack([hcos, -hsin]), jnp.stack([hsin, hcos])]))
    return jnp.stack(result)


def packed_rows(left_rows, right_rows, left_all, row_start):
    real_sums = jnp.einsum("cif,cjf->cij", left_rows, left_all, preferred_element_type=jnp.float32)
    imag_sums = jnp.einsum("cif,cjf->cij", right_rows, left_all, preferred_element_type=jnp.float32)
    row_index = row_start + jnp.arange(left_rows.shape[1])
    col_index = jnp.arange(left_all.shape[1])
    upper = row_index[:, None] <= col_index[None, :]
    return jnp.where(upper[None], real_sums, imag_sums)


def local(voltages, gains):
    coarse = voltages.shape[1]
    local_inputs = voltages.shape[2]
    samples = voltages.shape[3]
    frames = samples // FINE
    window = prototype(TAPS, FINE)
    filters = kernels(window, FINE)
    filter_table = jnp.transpose(filters, (1, 0, 3, 2, 4))
    filter_high = filter_table.astype(jnp.bfloat16)
    filter_low = (filter_table - filter_high.astype(jnp.float32)).astype(jnp.bfloat16)
    padded = jnp.pad(voltages, ((0, 0), (0, 0), (0, 0), (0, (TAPS - 1) * FINE)))
    stacked = jnp.stack(
        [padded[..., tap_index * FINE : tap_index * FINE + samples] for tap_index in range(TAPS)],
        axis=1,
    )
    stacked = stacked.reshape(2, TAPS, coarse, local_inputs, frames, FINE)
    spectra = jnp.einsum(
        "atcnmp,atpbk->bcknm", stacked, filter_high, preferred_element_type=jnp.float32
    )
    spectra = spectra + jnp.einsum(
        "atcnmp,atpbk->bcknm", stacked, filter_low, preferred_element_type=jnp.float32
    )
    gain_real = jnp.swapaxes(gains[0], 1, 2)[:, :, :, None]
    gain_imag = jnp.swapaxes(gains[1], 1, 2)[:, :, :, None]
    real_part = spectra[0] * gain_real - spectra[1] * gain_imag
    imag_part = spectra[0] * gain_imag + spectra[1] * gain_real
    outgoing = jnp.stack([real_part, imag_part]).astype(jnp.bfloat16)
    outgoing = outgoing.reshape(2, coarse * FINE, local_inputs, frames)
    turned = lax.all_to_all(outgoing, "inp", split_axis=1, concat_axis=2, tiled=True)
    inputs = turned.shape[2]
    span_count = lax.axis_size("span")
    row_count = inputs // span_count
    frame_scale = 1.0 / (span_count * frames)
    row_start = lax.axis_index("span") * row_count
    frame_piece = lax.all_gather(turned, "span", axis=3, tiled=True)
    left_all = jnp.concatenate([frame_piece[0], frame_piece[1]], axis=-1)
    own_rows = lax.dynamic_slice_in_dim(frame_piece, row_start, row_count, 2)
    left_rows = jnp.concatenate([own_rows[0], own_rows[1]], axis=-1)
    right_rows = jnp.concatenate([own_rows[1], -own_rows[0]], axis=-1)
    summed = packed_rows(left_rows, right_rows, left_all, row_start) * frame_scale
    return summed.astype(jnp.bfloat16)


def order_of(step, mine, coarse):
    if coarse == 4:
        high = (mine // 2 + 1 - step // 2) % 2
        low = (mine % 2 + (step + 1) // 2) % 2
        return 2 * high + low
    return (mine + step + 1) % coarse


def origin_of(step, mine, coarse):
    if coarse == 4:
        return order_of(step, mine, coarse)
    return (mine + coarse - (step + 1) % coarse) % coarse


def filter_rows(fine_count, tap_count, group):
    length = tap_count * fine_count
    offsets = np.arange(length, dtype=np.float64)
    shifted = (offsets - length / 2 + 0.5) / fine_count
    taper = 0.5 - 0.5 * np.cos(2.0 * np.pi * (offsets + 0.5) / length)
    window = np.sinc(shifted) * taper
    window = window / np.sqrt(np.sum(window * window))
    fine = np.arange(fine_count)
    angles = 2.0 * np.pi * ((offsets[None, :] * fine[:, None]) % fine_count) / fine_count
    hcos = window[None, :] * np.cos(angles)
    hsin = window[None, :] * np.sin(angles)
    span = group * fine_count + length
    rows = np.zeros((group, 2, fine_count, 2, span), np.float64)
    for frame in range(group):
        at = slice(frame * fine_count, frame * fine_count + length)
        rows[frame, 0, :, 0, at] = hcos
        rows[frame, 0, :, 1, at] = hsin
        rows[frame, 1, :, 0, at] = -hsin
        rows[frame, 1, :, 1, at] = hcos
    rows = rows.reshape(group * 2 * fine_count, 2 * span).astype(np.float32)
    high = rows.astype(jnp.bfloat16)
    low = (rows - high.astype(np.float32)).astype(jnp.bfloat16)
    return high, low


def products(dims, span, source, turned, result):
    ranks, _, _, local_inputs, frames, _, scale = dims
    rows = ranks * local_inputs // 2
    own_sources = ranks // 2
    depth = 2 * frames
    width = 2 * local_inputs

    def turn_over(part):
        @pl.loop(0, own_sources)
        def _(index):
            at = pl.ds(pl.multiple_of(index * local_inputs, local_inputs), local_inputs)
            where_real = pl.ds(pl.multiple_of(part * frames, frames), frames)
            where_imag = pl.ds(pl.multiple_of(depth + part * frames, frames), frames)
            real = source[part, span * own_sources + index, 0].T
            imag = source[part, span * own_sources + index, 1].T
            turned[0, at, where_real] = real
            turned[0, at, where_imag] = imag
            turned[1, at, where_real] = imag
            turned[1, at, where_imag] = -real

    def columns_of(pair):
        columns = []
        for side in range(2):
            other = pair * 2 + side
            columns.append(
                jnp.concatenate(
                    [source[part, other, piece] for piece in range(2) for part in range(2)], axis=0
                )
            )
        return jnp.concatenate(columns, axis=1)

    def multiply(index):
        @pl.loop(0, ranks // 4)
        def _(step):
            pair = (1 - span) * (ranks // 4) + step
            block = columns_of(pair)
            value = jnp.dot(turned[span], block, preferred_element_type=jnp.float32) * scale
            at = pl.multiple_of(pair * width, width)
            result[index, :, pl.ds(at, width)] = value.astype(jnp.bfloat16)

        @pl.loop(0, ranks // 4)
        def _(step):
            pair = span * (ranks // 4) + step
            block = columns_of(pair)
            real = jnp.dot(turned[0], block, preferred_element_type=jnp.float32)
            imag = jnp.dot(turned[1], block, preferred_element_type=jnp.float32)
            row = lax.broadcasted_iota(jnp.int32, (rows, width), 0)
            column = step * width + lax.broadcasted_iota(jnp.int32, (rows, width), 1)
            value = jnp.where(row <= column, real, imag) * scale
            at = pl.multiple_of(pair * width, width)
            result[index, :, pl.ds(at, width)] = value.astype(jnp.bfloat16)

    return turn_over, multiply


def finish_kernel(dims, done, last, vis, turned, obuf, outsem, osem):
    chunks = dims[2]
    span = lax.axis_index("span")
    turn_over, multiply = products(dims, span, last, turned, obuf)

    def give(channel):
        return pltpu.make_async_copy(done.at[channel], vis.at[channel], outsem.at[channel])

    for channel in range(chunks - 1):
        give(channel).start()
    for part in range(2):
        turn_over(part)
    multiply(0)
    result = pltpu.make_async_copy(obuf.at[0], vis.at[chunks - 1], osem)
    result.start()
    for channel in range(chunks - 1):
        give(channel).wait()
    result.wait()


def fused_kernel(
    dims, volt, gains_in, filters_in, vis, recv, last,
    send, xbuf, tbuf, filters, gains, bbuf, turned,
    xsem, fsem, gsem, ownsem, ssem, lssem, rsem, firstsem, lrsem, psend, precv, plsend, plrecv, bsem,
):
    ranks, coarse, chunks, local_inputs, frames, first, scale = dims
    halves = ranks // coarse
    samples = frames * FINE
    rest = frames - first
    many = chunks - 1
    ahead = min(3, many)
    early_far, early_near = min(3, ahead), min(3, ahead)
    beam = lax.axis_index("beam")
    me = lax.axis_index("inp")
    span = lax.axis_index("span")
    mine = me // halves
    my_half = me % halves
    here = (beam, me, 1 - span)

    def peer(step, turn):
        return order_of(step, mine, coarse) * halves + (my_half + turn) % halves

    def source(step, turn):
        return origin_of(step, mine, coarse) * halves + (my_half + turn) % halves

    peers = [(step, turn) for step in range(coarse) for turn in range(halves)]
    peers = [pair for pair in peers if pair != (coarse - 1, 0)]

    early = first * FINE + TAPS * FINE

    def load(step, slot, piece=None):
        block = order_of(step, mine, coarse)
        at = pl.ds(0, samples) if piece is None else (pl.ds(0, early), pl.ds(early, samples - early))[piece]
        return pltpu.make_async_copy(
            volt.at[:, block, :, at], xbuf.at[slot, :, :, at], xsem.at[slot if piece is None else 2 * piece]
        )

    load(0, 0, 0).start()
    take_filters = pltpu.make_async_copy(filters_in, filters, fsem)
    take_gains = pltpu.make_async_copy(gains_in, gains, gsem)
    take_filters.start()
    take_gains.start()

    barrier = pltpu.get_barrier_semaphore()
    for step, turn in peers:
        pl.semaphore_signal(barrier, inc=1, device_id=(beam, peer(step, turn), span), device_id_type=MESH)
    pl.semaphore_signal(barrier, inc=1, device_id=here, device_id_type=MESH)


    tail = jnp.zeros((2, local_inputs, TAPS * FINE), jnp.bfloat16)
    xbuf[0, :, :, pl.ds(samples, TAPS * FINE)] = tail
    xbuf[1, :, :, pl.ds(samples, TAPS * FINE)] = tail

    def remote(step, turn, src, dst, send_sem, recv_sem):
        return pltpu.make_async_remote_copy(
            src_ref=src, dst_ref=dst, send_sem=send_sem, recv_sem=recv_sem,
            device_id=(beam, peer(step, turn), span), device_id_type=MESH,
        )

    def early_of(step):
        return early_far if 2 * step < coarse else early_near

    def span_of(step):
        return pl.ds(first, rest) if step == 0 else pl.ds(0, frames)

    def outgoing(step, turn, chunk):
        other, at = peer(step, turn), span_of(step)
        return remote(
            step, turn, send.at[other, chunk, :, at], recv.at[span, chunk, me, :, at],
            ssem.at[other], rsem.at[chunk, me],
        )

    def outgoing_last(step, turn, at=None):
        other, at = peer(step, turn), span_of(step) if at is None else at
        return remote(
            step, turn, send.at[other, many, :, at], last.at[span, me, :, at], lssem.at[other], lrsem.at[me]
        )

    def outgoing_first(turn, at):
        other = peer(0, turn)
        return remote(
            0, turn, send.at[other, pl.ds(0, many), :, at], recv.at[span, :, me, :, at],
            ssem.at[other], firstsem.at[me],
        )

    def sent(step, turn):
        other = peer(step, turn)
        return remote(
            step, turn, send.at[other, pl.ds(0, many)], recv.at[span, :, me], ssem.at[other], firstsem.at[me]
        )

    def incoming(step, turn, chunk):
        other, at = source(step, turn), span_of(step)
        return remote(
            step, turn, recv.at[span, chunk, other, :, at], recv.at[span, chunk, other, :, at],
            ssem.at[other], rsem.at[chunk, other],
        )

    def incoming_first(turn):
        other, at = source(0, turn), pl.ds(0, first)
        return remote(
            0, turn, recv.at[span, :, other, :, at], recv.at[span, :, other, :, at],
            ssem.at[other], firstsem.at[other],
        )

    def incoming_last(other):
        return remote(0, 0, last.at[span, other], last.at[span, other], lssem.at[other], lrsem.at[other])

    def across(ref, send_sem, recv_sem):
        return pltpu.make_async_remote_copy(
            src_ref=ref, dst_ref=ref, send_sem=send_sem, recv_sem=recv_sem,
            device_id=here, device_id_type=MESH,
        )

    def channelize(slot, start, count):
        @pl.loop(0, count // 8, unroll=2)
        def _(pair):
            base = pl.multiple_of(start * FINE + pair * (8 * FINE), 4 * FINE)
            pieces = []
            for part in range(2):
                at = base + part * 4 * FINE
                at = pl.multiple_of(at, 4 * FINE)
                pieces.append(
                    jnp.concatenate(
                        [xbuf[slot, 0, :, pl.ds(at, 8 * FINE)], xbuf[slot, 1, :, pl.ds(at, 8 * FINE)]],
                        axis=1,
                    )
                )
            both = jnp.concatenate(pieces, axis=0)
            contract = (((1,), (1,)), ((), ()))
            got = lax.dot_general(filters[0], both, contract, preferred_element_type=jnp.float32)
            got = got + lax.dot_general(filters[1], both, contract, preferred_element_type=jnp.float32)
            at = pl.multiple_of(pair * (16 * FINE), 16 * FINE)
            tbuf[pl.ds(at, 8 * FINE), :] = got[:, :local_inputs]
            tbuf[pl.ds(at + 8 * FINE, 8 * FINE), :] = got[:, local_inputs:]

    def weigh(step, turn, start, count):
        block = order_of(step, mine, coarse)
        half = (my_half + turn) % halves
        other = peer(step, turn)

        @pl.loop(0, chunks, unroll=2)
        def _(chunk):
            fine = half * chunks + chunk
            real = tbuf[pl.ds(fine, count, stride=2 * FINE), :]
            imag = tbuf[pl.ds(FINE + fine, count, stride=2 * FINE), :]
            gain_real = gains[0, block, pl.ds(fine, 1), :]
            gain_imag = gains[1, block, pl.ds(fine, 1), :]
            at = pl.ds(start, count)
            send[other, chunk, 0, at] = (real * gain_real - imag * gain_imag).astype(jnp.bfloat16)
            send[other, chunk, 1, at] = (real * gain_imag + imag * gain_real).astype(jnp.bfloat16)

    load(0, 0, 0).wait()
    take_filters.wait()
    load(0, 0, 1).start()
    load(1, 1).start()
    for begin in range(0, first, first // 2):
        channelize(0, begin, first // 2)
        if begin == 0:
            take_gains.wait()
        for turn in range(halves):
            weigh(0, turn, begin, first // 2)
            if (begin, turn) == (0, 0):
                pl.semaphore_wait(barrier, len(peers) + 1)
            if (0, turn) in peers:
                at = pl.ds(begin, first // 2)
                outgoing_first(turn, at).start()
                outgoing_last(0, turn, at).start()
    for step in range(coarse):
        slot = step % 2
        start = first if step == 0 else 0
        if step == 0:
            load(0, 0, 1).wait()
        else:
            load(step, slot).wait()
        channelize(slot, start, frames - start)
        if step + 2 < coarse:
            load(step + 2, slot).start()
        for turn in range(halves):
            weigh(step, turn, start, frames - start)
            if (step, turn) in peers:

                for chunk in range(early_of(step)):
                    outgoing(step, turn, chunk).start()
            else:
                own = pltpu.make_async_copy(send.at[me, pl.ds(0, many)], recv.at[span, :, me], ownsem.at[0])
                own_last = pltpu.make_async_copy(send.at[me, many], last.at[span, me], ownsem.at[1])
                own.start()
                own_last.start()
    for chunk in range(ahead):
        for step, turn in peers:
            if chunk >= early_of(step):
                outgoing(step, turn, chunk).start()
    own.wait()
    own_last.wait()

    for turn in range(halves):
        if (0, turn) in peers:
            incoming_first(turn).wait_recv()

    def forward(chunk):
        return across(recv.at[span, chunk], psend.at[0], precv.at[chunk])

    def backward(chunk):
        return across(recv.at[1 - span, chunk], psend.at[0], precv.at[chunk])

    def fetch(chunk, part):
        return pltpu.make_async_copy(recv.at[part, chunk], bbuf.at[part], bsem.at[part])

    turn_over, multiply = products(dims, span, bbuf, turned, vis)

    @pl.loop(0, many)
    def _(chunk):
        for step, turn in peers:
            incoming(step, turn, chunk).wait_recv()

        @pl.when(chunk + ahead < many)
        def _():
            for step, turn in peers:
                outgoing(step, turn, chunk + ahead).start()

        @pl.when(chunk + ahead == many)
        def _():
            for step, turn in peers:
                outgoing_last(step, turn).start()

        forward(chunk).start()
        fetch(chunk, span).start()
        fetch(chunk, span).wait()
        turn_over(span)
        backward(chunk).wait_recv()
        fetch(chunk, 1 - span).start()
        fetch(chunk, 1 - span).wait()
        turn_over(1 - span)
        multiply(chunk)

    def forward_last(other):
        return across(last.at[span, other], plsend.at[other], plrecv.at[other])

    def backward_last(other):
        return across(last.at[1 - span, other], plsend.at[other], plrecv.at[other])

    inner = (mine // 2 + mine % 2) % 2
    pairs = [(source(0, turn), source(1, turn)) for turn in range(halves)]
    final = [source(step, turn) for step, turn in peers if step > 1]
    final += [inner * one + (1 - inner) * other for one, other in pairs]
    final += [(1 - inner) * one + inner * other for one, other in pairs]
    forward_last(me).start()
    for other in final:
        incoming_last(other).wait_recv()
        forward_last(other).start()
    for step, turn in peers:
        sent(step, turn).wait_send()
        outgoing_last(step, turn, pl.ds(0, frames)).wait_send()
    across(recv.at[span], psend.at[0], precv.at[0]).wait_send()
    for other in [me] + final:
        forward_last(other).wait_send()
        backward_last(other).wait_recv()


def fused(voltages, gains):
    coarse, local_inputs, samples = voltages.shape[1:]
    ranks = lax.axis_size("inp")
    frames = samples // FINE
    halves = ranks // coarse
    chunks = FINE // halves
    rows = ranks * local_inputs // 2
    columns = ranks * local_inputs
    first = 32
    filters = jnp.asarray(np.stack(filter_rows(FINE, TAPS, 4)))
    gain_rows = jnp.swapaxes(gains, 2, 3)
    scale = 1.0 / (2 * frames)
    dims = (ranks, coarse, chunks, local_inputs, frames, first, scale)
    bf16 = jnp.bfloat16
    anywhere = pl.BlockSpec(memory_space=pl.ANY)
    inside = pl.BlockSpec(memory_space=pltpu.VMEM)
    flops = 4 * chunks * rows * columns * 4 * frames
    done, _, last = pl.pallas_call(
        functools.partial(fused_kernel, dims),
        out_shape=(
            pltpu.VMEM((chunks - 1, rows, columns), bf16),
            jax.ShapeDtypeStruct((2, chunks - 1, ranks, 2, frames, local_inputs), bf16),
            pltpu.VMEM((2, ranks, 2, frames, local_inputs), bf16),
        ),
        in_specs=[anywhere, anywhere, anywhere],
        out_specs=(inside, anywhere, inside),
        scratch_shapes=[
            pltpu.VMEM((ranks, chunks, 2, frames, local_inputs), bf16),
            pltpu.VMEM((2, 2, local_inputs, samples + TAPS * FINE), bf16),
            pltpu.VMEM((frames * 2 * FINE, local_inputs), jnp.float32),
            pltpu.VMEM(filters.shape, bf16),
            pltpu.VMEM(gain_rows.shape, jnp.float32),
            pltpu.VMEM((2, ranks, 2, frames, local_inputs), bf16),
            pltpu.VMEM((2, rows, 4 * frames), bf16),
            pltpu.SemaphoreType.DMA((3,)),
            pltpu.SemaphoreType.DMA,
            pltpu.SemaphoreType.DMA,
            pltpu.SemaphoreType.DMA((2,)),
            pltpu.SemaphoreType.DMA((ranks,)),
            pltpu.SemaphoreType.DMA((ranks,)),
            pltpu.SemaphoreType.DMA((chunks - 1, ranks)),
            pltpu.SemaphoreType.DMA((ranks,)),
            pltpu.SemaphoreType.DMA((ranks,)),
            pltpu.SemaphoreType.DMA((1,)),
            pltpu.SemaphoreType.DMA((chunks - 1,)),
            pltpu.SemaphoreType.DMA((ranks,)),
            pltpu.SemaphoreType.DMA((ranks,)),
            pltpu.SemaphoreType.DMA((2,)),
        ],
        compiler_params=pltpu.CompilerParams(
            collective_id=0, has_side_effects=True, vmem_limit_bytes=44 * 1024 * 1024
        ),
        cost_estimate=pl.CostEstimate(flops=flops, bytes_accessed=2 * voltages.size * 8, transcendentals=0),
    )(voltages, gain_rows, filters)
    done = pltpu.with_memory_space_constraint(done, pltpu.VMEM)
    last = pltpu.with_memory_space_constraint(last, pltpu.VMEM)
    return pl.pallas_call(
        functools.partial(finish_kernel, dims),
        out_shape=jax.ShapeDtypeStruct((chunks, rows, columns), bf16),
        in_specs=[inside, inside],
        out_specs=anywhere,
        scratch_shapes=[
            pltpu.VMEM((2, rows, 4 * frames), bf16),
            pltpu.VMEM((1, rows, columns), bf16),
            pltpu.SemaphoreType.DMA((chunks - 1,)),
            pltpu.SemaphoreType.DMA,
        ],
        compiler_params=pltpu.CompilerParams(vmem_limit_bytes=24 * 1024 * 1024),
    )(done, last)


def vmem_needed(coarse, local_inputs, samples, ranks):
    frames = samples // FINE
    chunks = FINE * coarse // ranks
    spectra = 4 * frames * local_inputs
    columns = ranks * local_inputs
    kept = chunks * columns * columns + 2 * ranks * spectra
    sending = ranks * chunks * spectra
    sampled = 8 * local_inputs * (samples + TAPS * FINE)
    channelized = frames * 2 * FINE * local_inputs * 4
    correlated = 2 * ranks * spectra + columns * 4 * frames * 2
    return kept, sending + sampled + channelized + correlated


def chosen(voltages, gains):
    coarse, local_inputs, samples = voltages.shape[1:]
    ranks, spans = lax.axis_size("inp"), lax.axis_size("span")
    fits = (
        spans == 2
        and local_inputs % 128 == 0
        and coarse > 2
        and ranks % coarse == 0
        and ranks % 4 == 0
        and FINE % (ranks // coarse) == 0
        and samples % (16 * FINE) == 0
        and samples >= 64 * FINE
    )
    if fits:
        kept, working = vmem_needed(coarse, local_inputs, samples, ranks)
        fits = kept <= 18 * 1024 * 1024 and working <= 42 * 1024 * 1024
    return fused(voltages, gains) if fits else local(voltages, gains)


def solution(mesh):
    placed = (P(None, "beam", "inp", "span"), P(None, "beam", "inp", None))
    return jax.shard_map(
        chosen,
        mesh=mesh,
        in_specs=placed,
        out_specs=P(("beam", "inp"), "span", None),
        check_vma=False,
    )
```
